128 devices in a mesh: tiles: 16 (over y, z), lag: 8 (over x, core).
Axes of the slice: x: 4, y: 4, z: 4, core: 2. Of those that a mesh axis runs over, the one named last changes fastest.
Arguments:
- spectra: bfloat16 [32, 2, 2, 128, 8192], P('tiles', None, None, None, 'lag'), may hold values from -6 to 6
- requests: int32 [16, 6], replicated, may hold values from 0 to 31, as said below
- pairs: int32 [16, 3, 2], P('tiles'), may hold values from 0 to 5, as said below
- counts: int32 [16], P('tiles'), may hold values from 2 to 3, as said below
Outputs:
- stacked_lags: float32 [48, 64, 128, 128], P('tiles', 'lag')
The draws below stay inside these ranges and needn't reach their ends.
Inputs may be any that keep to these rules, and one draw needn't show every extreme that they name: Block b is held by index b // 2 of tiles; each row of requests names 6 blocks held by 6 different indices. Each row's 3 entries are pairs (i, j) of request slots with i < j that together use every request slot once. The first counts[d] slots of row d are live, the others give zeros; some index has 3.
All inputs are finite; a program needn't handle non-finite values.
Results may differ from the reference program's by a relative error of at most 0.012.
Values may be sent and summed in bfloat16 or wider, within the bound.
A program may use at most 128 MiB of HBM per device.

```python
import math
import jax
import jax.numpy as jnp
from jax import lax

CH = 128
F = 8192
W = 2
BPD = 2
NEED = 6
TMAX = 3
LAGS = 64
FBLK = 128
NB = 32
TSLOTS = 48
N_TILES = 16
N_LAG = 8


def draw_requests(key, part):
    row_keys = jax.random.split(jax.random.fold_in(key, 11), N_TILES)

    def one_row(row_key):
        owner_key, local_key = jax.random.split(row_key)
        owners = jax.random.permutation(owner_key, N_TILES)[:NEED]
        inside = jax.random.randint(local_key, (NEED,), 0, BPD)
        return (owners * BPD + inside).astype(jnp.int32)
    return jax.vmap(one_row)(row_keys)


def draw_pairs(key, part):
    row_keys = jax.random.split(jax.random.fold_in(key, 23), N_TILES)

    def one_row(row_key):
        order = jax.random.permutation(row_key, NEED).astype(jnp.int32).reshape(TMAX, 2)
        lower = jnp.minimum(order[:, 0], order[:, 1])
        upper = jnp.maximum(order[:, 0], order[:, 1])
        return jnp.stack([lower, upper], axis=1)
    return jax.vmap(one_row)(row_keys).astype(jnp.int32)


def draw_counts(key, part):
    first_key, second_key = jax.random.split(jax.random.fold_in(key, 37))
    short_one = (jax.random.randint(first_key, (N_TILES,), 0, 4) == 0).astype(jnp.int32)
    loads = TMAX - short_one
    busiest = jax.random.randint(second_key, (), 0, N_TILES)
    return loads.at[busiest].set(TMAX).astype(jnp.int32)


def block_scale(own_key, dims, cuts, low, high):
    def one(position, shards_of):
        steps = jax.random.uniform(jax.random.fold_in(jax.random.fold_in(own_key, 6), position), (shards_of,), jnp.float32, low / len(cuts), high / len(cuts))
        return jnp.repeat(jnp.exp(steps), dims[position] // shards_of).reshape((-1,) + (1,) * (len(dims) - position - 1))

    gain = one(*cuts[0])
    for cut in cuts[1:]:
        gain = gain * one(*cut)
    return gain


def noise(key, dims, scale, limit, cuts=(), held_as=jnp.bfloat16):
    drawn = jax.random.normal(key, dims, jnp.float32) * scale
    if len(cuts) > 0:
        drawn = block_scale(key, dims, cuts, -0.22, 0.18) * drawn
    return jnp.clip(drawn, min=-limit, max=limit).astype(held_as)


def setup_inputs(seed: int = 0) -> dict:
    splits = jax.random.split(jax.random.key(seed), 5)
    spectra = noise(splits[0], (NB, W, 2, CH, F), 1.0, 6.0, ((0, 16), (4, 8)))
    requests = draw_requests(jax.random.fold_in(splits[4], 71), 0)
    pairs = draw_pairs(jax.random.fold_in(splits[4], 71), 0)
    counts = draw_counts(jax.random.fold_in(splits[4], 71), 0)
    return dict(spectra=spectra, requests=requests, pairs=pairs, counts=counts)


def phase_table(freq_first, width):
    frequencies = freq_first + jnp.arange(width, dtype=jnp.int32)
    shifts = (jnp.arange(LAGS, dtype=jnp.int32) - LAGS // 2) % F
    phase_index = frequencies[:, None] * shifts[None, :] % F
    angles = phase_index.astype(jnp.float32) * (2.0 * math.pi / F)
    return jnp.concatenate([jnp.cos(angles), -jnp.sin(angles)], axis=0).astype(jnp.bfloat16)

def cross_block(left_part, right_part):
    left_wide = left_part.astype(jnp.float32)
    right_wide = right_part.astype(jnp.float32)
    real_part = lax.optimization_barrier(jnp.sum(left_wide[:, 0, :, None, :] * right_wide[:, 0, None, :, :] + left_wide[:, 1, :, None, :] * right_wide[:, 1, None, :, :], axis=0))
    imag_part = lax.optimization_barrier(jnp.sum(left_wide[:, 1, :, None, :] * right_wide[:, 0, None, :, :] - left_wide[:, 0, :, None, :] * right_wide[:, 1, None, :, :], axis=0))
    channels = left_part.shape[2]
    return jnp.concatenate([real_part, imag_part], axis=-1).reshape(channels * channels, -1).astype(jnp.bfloat16)

def band_sum(left_block, right_block, band_first):
    channels = left_block.shape[2]
    block_count = left_block.shape[-1] // FBLK

    def block_step(running, block_index):
        offset = block_index * FBLK
        left_part = lax.dynamic_slice_in_dim(left_block, offset, FBLK, 3)
        right_part = lax.dynamic_slice_in_dim(right_block, offset, FBLK, 3)
        stacked = cross_block(left_part, right_part).astype(jnp.float32)
        phases = phase_table(band_first + offset, FBLK).astype(jnp.float32)
        return (running + lax.dot_general(phases, stacked, (((0,), (1,)), ((), ())), preferred_element_type=jnp.float32), None)
    running = jnp.zeros((LAGS, channels * channels), jnp.float32)
    running, unused = lax.scan(block_step, running, jnp.arange(block_count, dtype=jnp.int32))
    return running

def reference(spectra, requests, pairs, counts):
    band_width = F // N_LAG
    norm_factor = 1.0 / math.sqrt(2.0 * W * F)

    def one_slot(slot_number):
        owner_row = slot_number // TMAX
        local_slot = slot_number % TMAX
        row_pairs = pairs[owner_row, local_slot]
        left_block = spectra[requests[owner_row, row_pairs[0]]]
        right_block = spectra[requests[owner_row, row_pairs[1]]]
        running = jnp.zeros((LAGS, CH * CH), jnp.float32)
        for band_index in range(N_LAG):
            band_first = band_index * band_width
            partial_sum = band_sum(left_block[..., band_first:band_first + band_width], right_block[..., band_first:band_first + band_width], band_first)
            rounded = lax.optimization_barrier((partial_sum * norm_factor).astype(jnp.bfloat16))
            running = running + rounded.astype(jnp.float32)
        is_live = local_slot < counts[owner_row]
        return jnp.where(is_live, running, jnp.zeros_like(running)).reshape(LAGS, CH, CH)
    return lax.map(one_slot, jnp.arange(TSLOTS, dtype=jnp.int32))
```

```python
import math

import jax
import jax.numpy as jnp
from jax import lax
from jax.experimental import pallas as pl
from jax.experimental.pallas import tpu as pltpu
from jax.sharding import PartitionSpec as P

F = 8192
W = 2
LAGS = 64
CH = 128
T1 = 8
T0 = 8
KC = 256


def phase_tables(first, width):
    freqs = first + jnp.arange(width, dtype=jnp.int32)
    coarse = T0 * jnp.arange(T1, dtype=jnp.int32) - LAGS // 2
    fine = -jnp.arange(T0, dtype=jnp.int32)

    def table(shifts):
        index = (freqs[None, :] * (shifts % F)[:, None]) % F
        angles = index.astype(jnp.float32) * (2.0 * math.pi / F)
        return jnp.stack([jnp.cos(angles), jnp.sin(angles)], axis=1)

    return table(coarse), table(fine)


def rotate(ref, window, table, count, dst, base):
    real = ref[window, 0].astype(jnp.float32)
    imag = ref[window, 1].astype(jnp.float32)
    for t in range(count):
        c = table[t, 0:1, :]
        s = table[t, 1:2, :]
        dst[t * CH : (t + 1) * CH, base : base + KC] = (real * c - imag * s).astype(jnp.bfloat16)
        dst[t * CH : (t + 1) * CH, base + KC : base + 2 * KC] = (real * s + imag * c).astype(
            jnp.bfloat16
        )


def pair_kernel(ids, a_ref, b_ref, coarse_ref, fine_ref, o_ref, u, v, acc):
    step = pl.program_id(1)

    @pl.when(step == 0)
    def _():
        acc[...] = jnp.zeros_like(acc)

    for w in range(W):
        rotate(a_ref, w, coarse_ref, T1, u, w * 2 * KC)
        rotate(b_ref, w, fine_ref, T0, v, w * 2 * KC)
    acc[...] += lax.dot_general(
        u[...], v[...], (((1,), (1,)), ((), ())), preferred_element_type=jnp.float32
    )

    @pl.when(step == pl.num_programs(1) - 1)
    def _():
        norm = 1.0 / math.sqrt(2.0 * W * F)
        for i in range(T1):
            for j in range(T0):
                block = acc[i * CH : (i + 1) * CH, j * CH : (j + 1) * CH]
                o_ref[i * T0 + j] = (block * norm).astype(jnp.bfloat16)


def pair_tiles(blocks, ids, coarse, fine):
    slots = ids.shape[0] // 2
    width = blocks.shape[-1]
    block = (None, W, 2, CH, KC)
    table = pl.BlockSpec((T1, 2, KC), lambda s, k, ids: (0, 0, k))
    grid_spec = pltpu.PrefetchScalarGridSpec(
        num_scalar_prefetch=1,
        grid=(slots, width // KC),
        in_specs=[
            pl.BlockSpec(block, lambda s, k, ids: (ids[2 * s], 0, 0, 0, k)),
            pl.BlockSpec(block, lambda s, k, ids: (ids[2 * s + 1], 0, 0, 0, k)),
            table,
            table,
        ],
        out_specs=pl.BlockSpec((None, LAGS, CH, CH), lambda s, k, ids: (s, 0, 0, 0)),
        scratch_shapes=[
            pltpu.VMEM((T1 * CH, 2 * W * KC), jnp.bfloat16),
            pltpu.VMEM((T0 * CH, 2 * W * KC), jnp.bfloat16),
            pltpu.VMEM((T1 * CH, T0 * CH), jnp.float32),
        ],
    )
    return pl.pallas_call(
        pair_kernel,
        grid_spec=grid_spec,
        out_shape=jax.ShapeDtypeStruct((slots, LAGS, CH, CH), jnp.bfloat16),
        name="pair_tiles",
    )(ids, blocks, blocks, coarse, fine)


def per_device(spectra, requests, pairs, counts):
    width = spectra.shape[-1]
    wanted = lax.dynamic_index_in_dim(requests, lax.axis_index("tiles"), 0, keepdims=False)
    shards = lax.all_gather(spectra, "tiles", axis=0, tiled=True)
    ids = wanted[pairs[0].reshape(-1)]
    coarse, fine = phase_tables(lax.axis_index("lag") * width, width)
    partial = pair_tiles(shards, ids, coarse, fine)
    live = jnp.arange(partial.shape[0]) < counts[0]
    summed = lax.psum_scatter(partial, "lag", scatter_dimension=1, tiled=True)
    return jnp.where(live[:, None, None, None], summed.astype(jnp.float32), 0.0)


def solution(mesh):
    placed = (P("tiles", None, None, None, "lag"), P(), P("tiles", None, None), P("tiles"))
    return jax.shard_map(
        per_device,
        mesh=mesh,
        in_specs=placed,
        out_specs=P("tiles", "lag", None, None),
        check_vma=False,
    )
```

```python
import math

import jax
import jax.numpy as jnp
import numpy as np
from jax import lax
from jax.experimental import pallas as pl
from jax.experimental.pallas import tpu as pltpu
from jax.sharding import PartitionSpec as P

MESH = pl.DeviceIdType.MESH
F = 8192
W = 2
LAGS = 64
CH = 128
BAND = 1024
NEED = 6
SLOTS = 3
SIDE = 4
T1 = 8
T0 = 8
CHUNKS = 4
KC = BAND // CHUNKS
NORM = 1.0 / math.sqrt(2.0 * W * F)


def phase_tables():
    freqs = np.arange(F, dtype=np.int64)
    coarse = T0 * np.arange(T1) - LAGS // 2
    fine = -np.arange(T0)

    def table(shifts):
        angles = (freqs[None, :] * shifts[:, None] % F) * (2.0 * math.pi / F)
        both = np.stack([np.cos(angles), np.sin(angles)], axis=1).astype(np.float32)
        return both.reshape(8, 2, F // BAND, BAND).transpose(2, 0, 1, 3)

    return np.stack([table(coarse), table(fine)], axis=1)


def pick(flags, values):
    total = jnp.int32(0)
    for flag, value in zip(flags, values, strict=True):
        total = total + jnp.where(flag, value, 0)
    return total


def request_plan(req_ref, node, along, across, by_y):
    rel, index = [], []
    for q in range(NEED):
        block = req_ref[node, q]
        holder = lax.div(block, 2)
        hy, hz = lax.div(holder, SIDE), lax.rem(holder, SIDE)
        h_along, h_across = (hy, hz) if by_y else (hz, hy)
        rel.append(lax.rem(h_along - along + SIDE, SIDE))
        index.append(2 * lax.rem(h_across - across + SIDE, SIDE) + lax.rem(block, 2))
    rank = []
    for q in range(NEED):
        total = jnp.int32(0)
        for earlier in range(q):
            total = total + jnp.where(rel[earlier] == rel[q], 1, 0)
        rank.append(total)
    n1 = pick([r == 1 for r in rel], [1] * NEED)
    n2 = pick([r == 2 for r in rel], [1] * NEED)
    plus = jnp.minimum(jnp.minimum(n2, 2), 4 - n1)
    return rel, index, rank, plus, n2 - plus


def kernel(*args):
    req_ref, pairs_ref, x_hbm, tab_hbm, o_ref = args[:5]
    rest = list(args[5:])

    def take(count):
        taken, rest[:count] = rest[:count], []
        return taken

    R = [take(CHUNKS) for _ in range(W)]
    FR = [take(CHUNKS) for _ in range(W)]
    TR = [take(CHUNKS) for _ in range(W)]
    FS = [take(2) for _ in range(W)]
    TS = [take(2) for _ in range(W)]
    tab, ab, u, v, acc, loc = take(6)
    PS, PR, S, XR, XS, YR = (take(SLOTS) for _ in range(6))
    local_sem, tab_sem, s1, r1, s1b, r1b, st, rt, sf, rf, sp, rp, sx, rx = take(14)

    me, lag = lax.axis_index("tiles"), lax.axis_index("lag")
    y, z = lax.div(me, SIDE), lax.rem(me, SIDE)
    x, core = lax.div(lag, 2), lax.rem(lag, 2)

    def shift(a, by):
        return lax.rem(a + by + SIDE, SIDE)

    def at(by_y, by):
        return (shift(y, by) * SIDE + z, lag) if by_y else (y * SIDE + shift(z, by), lag)

    def along_x(by):
        return (me, shift(x, by) * 2 + core)

    partner = (me, 2 * x + 1 - core)

    tables = pltpu.make_async_copy(tab_hbm.at[lag], tab, tab_sem)
    loads = {}
    for c in range(CHUNKS):
        for w in range(W):
            loads[c, w] = pltpu.make_async_copy(
                x_hbm.at[:, w, :, :, pl.ds(c * KC, KC)], R[w][c].at[0:2], local_sem.at[c, w]
            )
            loads[c, w].start()
    tables.start()
    barrier = pltpu.get_barrier_semaphore()
    friends = [at(True, -1), at(True, 1), at(False, -1), at(False, 1)]
    friends += [along_x(-1), along_x(1), partner]
    for friend in friends:
        pl.semaphore_signal(barrier, inc=1, device_id=friend, device_id_type=MESH)
    pl.semaphore_wait(barrier, len(friends))

    def remote(src, dst, send, recv, to):
        copy = pltpu.make_async_remote_copy(
            src_ref=src, dst_ref=dst, send_sem=send, recv_sem=recv, device_id=to, device_id_type=MESH
        )
        copy.start()
        return copy

    first, second, transit, final = {}, {}, {}, {}

    def start_first(c):
        for w in range(W):
            loads[c, w].wait()
            for k, (by, slot) in enumerate(((-1, 1), (1, 3))):
                for b in (k, 1 - k):
                    first[c, w, k, b] = remote(
                        R[w][c].at[b],
                        R[w][c].at[2 * slot + b],
                        s1.at[c, w, k, b],
                        r1.at[c, w, k, b],
                        at(w == 1, by),
                    )

    def start_second(c):
        for w in range(W):
            for k, (by, slot) in enumerate(((-1, 1), (1, 3))):
                first[c, w, k, k].wait_recv()
                second[c, w, k] = remote(
                    R[w][c].at[2 * slot + k],
                    R[w][c].at[4 + k],
                    s1b.at[c, w, k],
                    r1b.at[c, w, k],
                    at(w == 1, by),
                )

    start_first(0)
    start_first(1)

    finals, transits, passing = {}, {}, {}
    for w in range(W):
        along, across = (y, z) if w == 0 else (z, y)
        by_y = w == 0

        def plan(by):
            there = shift(along, by)
            node = there * SIDE + across if by_y else across * SIDE + there
            return request_plan(req_ref, node, there, across, by_y)

        for k, (by, mine) in enumerate(((-1, 1), (1, 3))):
            rel, index, rank, plus, minus = plan(by)
            for j in range(4):
                finals[w, k, j] = pick(
                    [(a == mine) & (b == j) for a, b in zip(rel, rank, strict=True)], index
                )
            passing[w, k] = (plus, minus)[k]
        rel, index, rank, plus, minus = plan(2)
        for j in range(2):
            transits[w, 0, j] = pick(
                [(a == 2) & (b < plus) & (b == j) for a, b in zip(rel, rank, strict=True)], index
            )
            transits[w, 1, j] = pick(
                [(a == 2) & (b - plus == j) for a, b in zip(rel, rank, strict=True)], index
            )
        rel, index, rank, plus, minus = plan(0)
        for q in range(NEED):
            r = rank[q]
            far = jnp.where(r < plus, 8 + 3 - r, 12 + 3 - (r - plus))
            where = jnp.where(rel[q] == 2, far, jnp.where(rel[q] == 3, 12 + r, 8 + r))
            loc[w, q] = jnp.where(rel[q] == 0, index[q], where)

    def start_third(c):
        half = c % 2
        if c >= 2:
            for w in range(W):
                for k in range(2):
                    transit[c - 2, w, k].wait_send()
                    final[c - 2, w, k, 0].wait_send()
                    final[c - 2, w, k, 1].wait_send()
        for w in range(W):
            for k in range(2):
                first[c, w, k, 1 - k].wait_recv()
                second[c, w, k].wait_recv()
        for w in range(W):
            for k in range(2):
                for j in range(2):
                    TS[w][half][k, j] = R[w][c][transits[w, k, j]]
        for w in range(W):
            for k, by in enumerate((-1, 1)):
                transit[c, w, k] = remote(
                    TS[w][half].at[k], TR[w][c].at[k], st.at[c, w, k], rt.at[c, w, k], at(w == 0, by)
                )
        for w in range(W):
            for k in range(2):
                for j in range(2):
                    FS[w][half][k, j] = R[w][c][finals[w, k, j]]
        for w in range(W):
            for k, by in enumerate((-1, 1)):
                final[c, w, k, 0] = remote(
                    FS[w][half].at[k, 0:2],
                    FR[w][c].at[4 * k : 4 * k + 2],
                    sf.at[c, w, k, 0],
                    rf.at[c, w, k, 0],
                    at(w == 0, by),
                )

    def start_fourth(c):
        half = c % 2
        for w in range(W):
            for k in range(2):
                transit[c, w, k].wait_recv()
        for w in range(W):
            for k in range(2):
                for j in (2, 3):
                    direct = R[w][c][finals[w, k, j]]
                    passed = TR[w][c][k, 3 - j]
                    FS[w][half][k, j] = jnp.where(passing[w, k] > 3 - j, passed, direct)
        for w in range(W):
            for k, by in enumerate((-1, 1)):
                final[c, w, k, 1] = remote(
                    FS[w][half].at[k, 2:4],
                    FR[w][c].at[4 * k + 2 : 4 * k + 4],
                    sf.at[c, w, k, 1],
                    rf.at[c, w, k, 1],
                    at(w == 0, by),
                )

    def wait_finals(c):
        for w in range(W):
            for k in range(2):
                final[c, w, k, 0].wait_recv()
                final[c, w, k, 1].wait_recv()

    def compute(c, s):
        for w in range(W):
            for side in range(2):
                where = loc[w, pairs_ref[0, s, side]]
                i = lax.rem(where, 8)
                block = jnp.where(where < 8, R[w][c][i], FR[w][c][i])
                ab[side, w] = block.astype(jnp.float32)

        def rotate(t, carry):
            rows = pl.ds(pl.multiple_of(t * CH, CH), CH)
            for side, dst in enumerate((u, v)):
                cos = tab[side, t, 0:1, c * KC : (c + 1) * KC]
                sin = tab[side, t, 1:2, c * KC : (c + 1) * KC]
                for w in range(W):
                    real, imag = ab[side, w, 0], ab[side, w, 1]
                    base = 2 * w * KC
                    dst[rows, base : base + KC] = (real * cos - imag * sin).astype(jnp.bfloat16)
                    dst[rows, base + KC : base + 2 * KC] = (real * sin + imag * cos).astype(
                        jnp.bfloat16
                    )
            return carry

        lax.fori_loop(0, T1, rotate, 0)

        def multiply(n, carry):
            cols = pl.ds(pl.multiple_of(n * 256, 256), 256)
            part = lax.dot_general(
                u[...], v[cols, :], (((1,), (1,)), ((), ())), preferred_element_type=jnp.float32
            )
            if c == 0:
                acc[s, :, cols] = part
            else:
                acc[s, :, cols] += part
            return carry

        lax.fori_loop(0, T0 * CH // 256, multiply, 0)

    def compute_all(c):
        def one(s, carry):
            compute(c, s)
            return carry

        lax.fori_loop(0, SLOTS, one, 0)

    pair_copy, x_copy = {}, {}

    def rows_of(there, which):
        return pl.ds(pl.multiple_of((2 * there + which) * CH, CH), CH)

    def send_pair(s):
        for there in range(SIDE):
            PS[s][there] = (acc[s, rows_of(there, 1 - core), :] * NORM).astype(jnp.bfloat16)
        pair_copy[s] = remote(PS[s], PR[s], sp.at[s], rp.at[s], partner)

    HALF = T0 * CH // 2
    lo, hi = slice(0, HALF), slice(HALF, 2 * HALF)

    def chip_sum(s):
        pair_copy[s].wait_recv()

        def total(by):
            there = shift(x, by)
            mine = acc[s, rows_of(there, core), :] * NORM
            return mine + PR[s][there].astype(jnp.float32)

        far = total(2).astype(jnp.bfloat16)
        XS[s][0, 0] = far[:, lo]
        XS[s][1, 0] = far[:, hi]
        for k, by in enumerate((1, -1)):
            x_copy[s, k, 0] = remote(
                XS[s].at[k, 0], XR[s].at[k, 0], sx.at[s, k, 0], rx.at[s, k, 0], along_x(by)
            )
        for k, by in enumerate((1, -1)):
            near = total(by)
            relayed, own = (lo, hi) if k == 0 else (hi, lo)
            YR[s][k] = near[:, relayed]
            XS[s][k, 1] = near[:, own].astype(jnp.bfloat16)
            x_copy[s, k, 1] = remote(
                XS[s].at[k, 1], XR[s].at[k, 1], sx.at[s, k, 1], rx.at[s, k, 1], along_x(by)
            )
        S[s][...] = total(0)

    def relay(s):
        for k, by in enumerate((1, -1)):
            x_copy[s, k, 0].wait_recv()
            XS[s][k, 2] = (YR[s][k] + XR[s][k, 0].astype(jnp.float32)).astype(jnp.bfloat16)
            x_copy[s, k, 2] = remote(
                XS[s].at[k, 2], XR[s].at[k, 2], sx.at[s, k, 2], rx.at[s, k, 2], along_x(by)
            )

    def finish(s):
        for k in range(2):
            x_copy[s, k, 1].wait_recv()
            x_copy[s, k, 2].wait_recv()
        low = S[s][:, lo] + XR[s][0, 2].astype(jnp.float32) + XR[s][1, 1].astype(jnp.float32)
        high = S[s][:, hi] + XR[s][0, 1].astype(jnp.float32) + XR[s][1, 2].astype(jnp.float32)
        for t in range(T0 // 2):
            o_ref[s, t] = low[:, t * CH : (t + 1) * CH]
            o_ref[s, T0 // 2 + t] = high[:, t * CH : (t + 1) * CH]

    tables.wait()
    start_second(0)
    start_first(2)
    for c in range(CHUNKS):
        start_third(c)
        start_fourth(c)
        if c + 1 < CHUNKS:
            start_second(c + 1)
        if c + 3 < CHUNKS:
            start_first(c + 3)
        if c > 0:
            wait_finals(c - 1)
            compute_all(c - 1)
    last = CHUNKS - 1
    wait_finals(last)
    compute(last, 0)
    send_pair(0)
    compute(last, 1)
    send_pair(1)
    chip_sum(0)
    compute(last, 2)
    send_pair(2)
    relay(0)
    chip_sum(1)
    relay(1)
    chip_sum(2)
    finish(0)
    relay(2)
    finish(1)
    finish(2)

    for copy in list(first.values()) + list(second.values()):
        copy.wait_send()
    for c in (CHUNKS - 2, CHUNKS - 1):
        for w in range(W):
            for k in range(2):
                transit[c, w, k].wait_send()
                final[c, w, k, 0].wait_send()
                final[c, w, k, 1].wait_send()
    for copy in list(pair_copy.values()) + list(x_copy.values()):
        copy.wait_send()


def per_device(spectra, requests, pairs, counts, tables):
    bf16, f32 = jnp.bfloat16, jnp.float32
    vmem, dma = pltpu.VMEM, pltpu.SemaphoreType.DMA
    half = (2, CH, KC)
    scratch = [vmem((8, *half), bf16)] * (W * CHUNKS)
    scratch += [vmem((8, *half), bf16)] * (W * CHUNKS)
    scratch += [vmem((2, 2, *half), bf16)] * (W * CHUNKS)
    scratch += [vmem((2, 4, *half), bf16)] * (W * 2)
    scratch += [vmem((2, 2, *half), bf16)] * (W * 2)
    scratch += [
        vmem((2, 8, 2, BAND), f32),
        vmem((2, W, 2, CH, KC), f32),
        vmem((T1 * CH, 2 * W * KC), bf16),
        vmem((T0 * CH, 2 * W * KC), bf16),
        vmem((SLOTS, T1 * CH, T0 * CH), f32),
        pltpu.SMEM((W, NEED), jnp.int32),
    ]
    scratch += [vmem((SIDE, CH, T0 * CH), bf16)] * (2 * SLOTS)
    scratch += [vmem((CH, T0 * CH), f32)] * SLOTS
    scratch += [vmem((2, 3, CH, T0 * CH // 2), bf16)] * (2 * SLOTS)
    scratch += [vmem((2, CH, T0 * CH // 2), f32)] * SLOTS
    scratch += [
        dma((CHUNKS, W)),
        dma,
        dma((CHUNKS, W, 2, 2)),
        dma((CHUNKS, W, 2, 2)),
        dma((CHUNKS, W, 2)),
        dma((CHUNKS, W, 2)),
        dma((CHUNKS, W, 2)),
        dma((CHUNKS, W, 2)),
        dma((CHUNKS, W, 2, 2)),
        dma((CHUNKS, W, 2, 2)),
        dma((SLOTS,)),
        dma((SLOTS,)),
        dma((SLOTS, 2, 3)),
        dma((SLOTS, 2, 3)),
    ]
    smem = pl.BlockSpec(memory_space=pltpu.SMEM)
    hbm = pl.BlockSpec(memory_space=pl.ANY)
    summed = pl.pallas_call(
        kernel,
        out_shape=jax.ShapeDtypeStruct((SLOTS, T0, CH, CH), f32),
        in_specs=[smem, smem, hbm, hbm],
        out_specs=pl.BlockSpec(memory_space=pltpu.VMEM),
        scratch_shapes=scratch,
        compiler_params=pltpu.CompilerParams(
            collective_id=0, has_side_effects=True, vmem_limit_bytes=67043328
        ),
        name="correlate",
    )(requests, pairs, spectra, tables)
    live = jnp.arange(SLOTS) < counts[0]
    return jnp.where(live[:, None, None, None], summed, 0.0)


def solution(mesh):
    placed = (P("tiles", None, None, None, "lag"), P(), P("tiles", None, None), P("tiles"), P())
    tables = phase_tables()
    mapped = jax.shard_map(
        per_device,
        mesh=mesh,
        in_specs=placed,
        out_specs=P("tiles", "lag", None, None),
        check_vma=False,
    )

    def run(spectra, requests, pairs, counts):
        return mapped(spectra, requests, pairs, counts, jnp.asarray(tables))

    return run
```

```python
import math

import jax
import jax.numpy as jnp
import numpy as np
from jax import lax
from jax.experimental import pallas as pl
from jax.experimental.pallas import tpu as pltpu
from jax.sharding import PartitionSpec as P

MESH = pl.DeviceIdType.MESH
F = 8192
W = 2
LAGS = 64
CH = 128
BAND = 1024
NEED = 6
SLOTS = 3
SIDE = 4
T1 = 8
T0 = 8
WIDTHS = (256, 256, 256, 128, 128)
STARTS = (0, 256, 512, 768, 896)
CHUNKS = len(WIDTHS)
LAST = CHUNKS - 1
BUFFER = (0, 1, 0, 2, 3)
BUFFER_WIDTHS = (256, 256, 128, 128)
BUFFERS = len(BUFFER_WIDTHS)
EARLY = (0, 3, 3, 3, 2)
NORM = 1.0 / math.sqrt(2.0 * W * F)


COARSE = T0 * np.arange(T1) - LAGS // 2
FINE = -np.arange(T0)


def phase_tables():
    freqs = np.arange(BAND, dtype=np.int64)

    def table(shifts):
        angles = (freqs[None, :] * shifts[:, None] % F) * (2.0 * math.pi / F)
        return np.stack([np.cos(angles), np.sin(angles)], axis=1)

    base = np.stack([table(COARSE), table(FINE)]).astype(np.float32)
    bands = np.arange(F // BAND, dtype=np.int64)
    turns = (bands[:, None] * BAND * FINE[None, :] % F) * (2.0 * math.pi / F)
    turn = np.stack([np.cos(turns), np.sin(turns)], axis=-1).astype(np.float32)
    return base, np.repeat(turn[..., None], 128, axis=-1)


def pick(flags, values):
    total = jnp.int32(0)
    for flag, value in zip(flags, values, strict=True):
        total = total + jnp.where(flag, value, 0)
    return total


def request_plan(req_ref, node, along, across, by_y):
    rel, index = [], []
    for q in range(NEED):
        block = req_ref[q, node]
        holder = lax.div(block, 2)
        hy, hz = lax.div(holder, SIDE), lax.rem(holder, SIDE)
        h_along, h_across = (hy, hz) if by_y else (hz, hy)
        rel.append(lax.rem(h_along - along + SIDE, SIDE))
        index.append(2 * lax.rem(h_across - across + SIDE, SIDE) + lax.rem(block, 2))
    rank = []
    for q in range(NEED):
        total = jnp.int32(0)
        for earlier in range(q):
            total = total + jnp.where(rel[earlier] == rel[q], 1, 0)
        rank.append(total)
    n1 = pick([r == 1 for r in rel], [1] * NEED)
    n2 = pick([r == 2 for r in rel], [1] * NEED)
    plus = jnp.minimum(jnp.minimum(n2, 2), 4 - n1)
    return rel, index, rank, plus, n2 - plus


def kernel(*args):
    req_ref, pairs_ref, counts_hbm, x_hbm, tab_hbm, turn_hbm, o_ref = args[:7]
    rest = list(args[7:])

    def take(count):
        taken, rest[:count] = rest[:count], []
        return taken

    R = [take(CHUNKS) for _ in range(W)]
    FR = [take(CHUNKS) for _ in range(W)]
    TR = [take(CHUNKS) for _ in range(W)]
    FS = [take(BUFFERS) for _ in range(W)]
    TS = [take(BUFFERS) for _ in range(W)]
    tab, turn, u, v, acc, loc, counts_ref = take(7)
    PS, PR, S, XR, XS, YR = (take(SLOTS) for _ in range(6))
    local_sem, tab_sem, turn_sem, count_sem, s1, r1, s1b, r1b, st, rt, sf, rf, sp, rp, sx, rx = take(16)

    me, lag = lax.axis_index("tiles"), lax.axis_index("lag")
    y, z = lax.div(me, SIDE), lax.rem(me, SIDE)
    x, core = lax.div(lag, 2), lax.rem(lag, 2)

    def shift(a, by):
        return lax.rem(a + by + SIDE, SIDE)

    def at(by_y, by):
        return (shift(y, by) * SIDE + z, lag) if by_y else (y * SIDE + shift(z, by), lag)

    def along_x(by):
        return (me, shift(x, by) * 2 + core)

    partner = (me, 2 * x + 1 - core)

    tables = pltpu.make_async_copy(tab_hbm, tab, tab_sem)
    turns = pltpu.make_async_copy(turn_hbm.at[lag], turn, turn_sem)
    loads = {}
    for c in range(CHUNKS):
        for w in range(W):
            loads[c, w] = pltpu.make_async_copy(
                x_hbm.at[:, w, :, :, pl.ds(STARTS[c], WIDTHS[c])], R[w][c].at[0:2], local_sem.at[c, w]
            )
            loads[c, w].start()
    tables.start()
    turns.start()
    live_count = pltpu.make_async_copy(counts_hbm, counts_ref, count_sem)
    live_count.start()
    barrier = pltpu.get_barrier_semaphore()
    friends = [at(True, -1), at(True, 1), at(False, -1), at(False, 1)]
    friends += [along_x(-1), along_x(1), partner]
    for friend in friends:
        pl.semaphore_signal(barrier, inc=1, device_id=friend, device_id_type=MESH)
    pl.semaphore_wait(barrier, len(friends))

    def remote(src, dst, send, recv, to):
        copy = pltpu.make_async_remote_copy(
            src_ref=src, dst_ref=dst, send_sem=send, recv_sem=recv, device_id=to, device_id_type=MESH
        )
        copy.start()
        return copy

    first, second, transit, final, arrival = {}, {}, {}, {}, {}

    def start_first(c):
        for w in range(W):
            loads[c, w].wait()
            for k, (by, slot) in enumerate(((-1, 1), (1, 3))):
                for b in (k, 1 - k):
                    first[c, w, k, b] = remote(
                        R[w][c].at[b],
                        R[w][c].at[2 * slot + b],
                        s1.at[c, w, k, b],
                        r1.at[c, w, k, b],
                        at(w == 1, by),
                    )

    def start_second(c):
        for w in range(W):
            for k, (by, slot) in enumerate(((-1, 1), (1, 3))):
                first[c, w, k, k].wait_recv()
                second[c, w, k] = remote(
                    R[w][c].at[2 * slot + k],
                    R[w][c].at[4 + k],
                    s1b.at[c, w, k],
                    r1b.at[c, w, k],
                    at(w == 1, by),
                )

    start_first(0)
    start_first(1)

    finals, transits, passing = {}, {}, {}
    for w in range(W):
        along, across = (y, z) if w == 0 else (z, y)
        by_y = w == 0

        def plan(by):
            there = shift(along, by)
            node = there * SIDE + across if by_y else across * SIDE + there
            return request_plan(req_ref, node, there, across, by_y)

        for k, (by, mine) in enumerate(((-1, 1), (1, 3))):
            rel, index, rank, plus, minus = plan(by)
            for j in range(4):
                finals[w, k, j] = pick(
                    [(a == mine) & (b == j) for a, b in zip(rel, rank, strict=True)], index
                )
            passing[w, k] = (plus, minus)[k]
        rel, index, rank, plus, minus = plan(2)
        for j in range(2):
            transits[w, 0, j] = pick(
                [(a == 2) & (b < plus) & (b == j) for a, b in zip(rel, rank, strict=True)], index
            )
            transits[w, 1, j] = pick(
                [(a == 2) & (b - plus == j) for a, b in zip(rel, rank, strict=True)], index
            )
        rel, index, rank, plus, minus = plan(0)
        for q in range(NEED):
            r = rank[q]
            far = jnp.where(r < plus, 8 + 3 - r, 12 + 3 - (r - plus))
            where = jnp.where(rel[q] == 2, far, jnp.where(rel[q] == 3, 12 + r, 8 + r))
            loc[w, q] = jnp.where(rel[q] == 0, index[q], where)

    def start_third(c):
        if BUFFER[c] in BUFFER[:c]:
            before = BUFFER.index(BUFFER[c])
            for w in range(W):
                for k in range(2):
                    transit.pop((before, w, k)).wait_send()
                    final.pop((before, w, k, 0)).wait_send()
                    final.pop((before, w, k, 1)).wait_send()
        for w in range(W):
            for k in range(2):
                first[c, w, k, 1 - k].wait_recv()
                second[c, w, k].wait_recv()
        for w in range(W):
            for k in range(2):
                for j in range(2):
                    TS[w][BUFFER[c]][k, j] = R[w][c][transits[w, k, j]]
        for w in range(W):
            for k, by in enumerate((-1, 1)):
                transit[c, w, k] = remote(
                    TS[w][BUFFER[c]].at[k], TR[w][c].at[k], st.at[c, w, k], rt.at[c, w, k], at(w == 0, by)
                )
        for w in range(W):
            for k in range(2):
                for j in range(2):
                    FS[w][BUFFER[c]][k, j] = R[w][c][finals[w, k, j]]
        for w in range(W):
            for k, by in enumerate((-1, 1)):
                final[c, w, k, 0] = arrival[c, w, k, 0] = remote(
                    FS[w][BUFFER[c]].at[k, 0:2],
                    FR[w][c].at[4 * k : 4 * k + 2],
                    sf.at[c, w, k, 0],
                    rf.at[c, w, k, 0],
                    at(w == 0, by),
                )

    def start_fourth(c):
        for w in range(W):
            for k in range(2):
                transit[c, w, k].wait_recv()
        for w in range(W):
            for k in range(2):
                for j in (2, 3):
                    direct = R[w][c][finals[w, k, j]]
                    passed = TR[w][c][k, 3 - j]
                    FS[w][BUFFER[c]][k, j] = jnp.where(passing[w, k] > 3 - j, passed, direct)
        for w in range(W):
            for k, by in enumerate((-1, 1)):
                final[c, w, k, 1] = arrival[c, w, k, 1] = remote(
                    FS[w][BUFFER[c]].at[k, 2:4],
                    FR[w][c].at[4 * k + 2 : 4 * k + 4],
                    sf.at[c, w, k, 1],
                    rf.at[c, w, k, 1],
                    at(w == 0, by),
                )

    def wait_finals(c):
        for w in range(W):
            for k in range(2):
                arrival[c, w, k, 0].wait_recv()
                arrival[c, w, k, 1].wait_recv()

    def turn_fine():
        for t in range(T0):
            cos, sin = tab[1, t, 0:1, :], tab[1, t, 1:2, :]
            c, m = turn[t, 0:1, 0:1], turn[t, 1:2, 0:1]
            tab[1, t, 0:1, :] = cos * c - sin * m
            tab[1, t, 1:2, :] = cos * m + sin * c

    STRIP = 32

    def compute(c, s):
        kc, first_col = WIDTHS[c], STARTS[c]
        cols = slice(first_col, first_col + kc)
        for w in range(W):
            for side, dst in enumerate((u, v)):
                where = loc[w, pairs_ref[0, side, s]]
                i = lax.rem(where, 8)
                for r in range(0, CH, STRIP):
                    rows = slice(r, r + STRIP)
                    block = jnp.where(where < 8, R[w][c][i, :, rows, :], FR[w][c][i, :, rows, :])
                    real, imag = block[0].astype(jnp.float32), block[1].astype(jnp.float32)
                    base = 2 * w * kc
                    for t in range(8):
                        cos = tab[side, t, 0:1, cols]
                        sin = tab[side, t, 1:2, cols]
                        out = slice(t * CH + r, t * CH + r + STRIP)
                        dst[out, base : base + kc] = (real * cos - imag * sin).astype(jnp.bfloat16)
                        dst[out, base + kc : base + 2 * kc] = (real * sin + imag * cos).astype(
                            jnp.bfloat16
                        )
        part = lax.dot_general(
            u[:, : 4 * kc],
            v[:, : 4 * kc],
            (((1,), (1,)), ((), ())),
            preferred_element_type=jnp.float32,
        )
        if c == 0:
            acc[s] = part
        else:
            acc[s] += part

    def compute_some(c, slots):
        def one(s, carry):
            compute(c, s)
            return carry

        lax.fori_loop(0, slots, one, 0)

    pair_copy, x_copy = {}, {}
    ORDER = (2, 1, -1, 0)

    def rows_of(there, which):
        return pl.ds(pl.multiple_of((2 * there + which) * CH, CH), CH)

    def send_pair(s):
        for n, by in enumerate(ORDER):
            block = acc[s, rows_of(shift(x, by), 1 - core), :] * NORM
            PS[s][n] = block.astype(jnp.bfloat16)
            pair_copy[s, n] = remote(
                PS[s].at[n], PR[s].at[n], sp.at[s, n], rp.at[s, n], partner
            )

    HALF = T0 * CH // 2
    lo, hi = slice(0, HALF), slice(HALF, 2 * HALF)

    def chip_sum(s):
        def total(by):
            n = ORDER.index(by)
            pair_copy[s, n].wait_recv()
            mine = acc[s, rows_of(shift(x, by), core), :] * NORM
            return mine + PR[s][n].astype(jnp.float32)

        far = total(2).astype(jnp.bfloat16)
        XS[s][0, 0] = far[:, lo]
        XS[s][1, 0] = far[:, hi]
        for k, by in enumerate((1, -1)):
            x_copy[s, k, 0] = remote(
                XS[s].at[k, 0], XR[s].at[k, 0], sx.at[s, k, 0], rx.at[s, k, 0], along_x(by)
            )
        for k, by in enumerate((1, -1)):
            near = total(by)
            relayed, own = (lo, hi) if k == 0 else (hi, lo)
            YR[s][k] = near[:, relayed]
            XS[s][k, 1] = near[:, own].astype(jnp.bfloat16)
            x_copy[s, k, 1] = remote(
                XS[s].at[k, 1], XR[s].at[k, 1], sx.at[s, k, 1], rx.at[s, k, 1], along_x(by)
            )
        S[s][...] = total(0)

    def relay(s):
        for k, by in enumerate((1, -1)):
            x_copy[s, k, 0].wait_recv()
            XS[s][k, 2] = (YR[s][k] + XR[s][k, 0].astype(jnp.float32)).astype(jnp.bfloat16)
            x_copy[s, k, 2] = remote(
                XS[s].at[k, 2], XR[s].at[k, 2], sx.at[s, k, 2], rx.at[s, k, 2], along_x(by)
            )

    def finish(s):
        for k in range(2):
            x_copy[s, k, 1].wait_recv()
            x_copy[s, k, 2].wait_recv()
        low = S[s][:, lo] + XR[s][0, 2].astype(jnp.float32) + XR[s][1, 1].astype(jnp.float32)
        high = S[s][:, hi] + XR[s][0, 1].astype(jnp.float32) + XR[s][1, 2].astype(jnp.float32)
        live = s < counts_ref[0]
        for t in range(T0 // 2):
            o_ref[s, t] = jnp.where(live, low[:, t * CH : (t + 1) * CH], 0.0)
            o_ref[s, T0 // 2 + t] = jnp.where(live, high[:, t * CH : (t + 1) * CH], 0.0)

    tables.wait()
    turns.wait()
    turn_fine()
    live_count.wait()
    start_second(0)
    start_first(2)
    for c in range(CHUNKS):
        start_third(c)
        if c > 0:
            wait_finals(c - 1)
            compute_some(c - 1, EARLY[c])
        start_fourth(c)
        if c + 1 < CHUNKS:
            start_second(c + 1)
        if c + 3 < CHUNKS:
            start_first(c + 3)
        if c > 0:
            for n in range(EARLY[c], SLOTS):
                compute(c - 1, n)
    last = LAST
    wait_finals(last)
    compute(last, 0)
    send_pair(0)
    compute(last, 1)
    send_pair(1)
    chip_sum(0)
    compute(last, 2)
    send_pair(2)
    relay(0)
    chip_sum(1)
    relay(1)
    chip_sum(2)
    finish(0)
    relay(2)
    finish(1)
    finish(2)

    for copy in list(first.values()) + list(second.values()):
        copy.wait_send()
    for copy in list(transit.values()) + list(final.values()):
        copy.wait_send()
    for copy in list(pair_copy.values()) + list(x_copy.values()):
        copy.wait_send()


def per_device(spectra, requests, pairs, counts, tables, turns):
    bf16, f32 = jnp.bfloat16, jnp.float32
    vmem, dma = pltpu.VMEM, pltpu.SemaphoreType.DMA
    scratch = []
    for lead in ((8,), (8,), (2, 2)):
        scratch += [vmem((*lead, 2, CH, width), bf16) for width in WIDTHS] * W
    for lead in ((2, 4), (2, 2)):
        scratch += [vmem((*lead, 2, CH, width), bf16) for width in BUFFER_WIDTHS] * W
    scratch += [
        vmem((2, 8, 2, BAND), f32),
        vmem((8, 2, 128), f32),
        vmem((T1 * CH, 2 * W * max(WIDTHS)), bf16),
        vmem((T0 * CH, 2 * W * max(WIDTHS)), bf16),
        vmem((SLOTS, T1 * CH, T0 * CH), f32),
        pltpu.SMEM((W, NEED), jnp.int32),
        pltpu.SMEM((1,), jnp.int32),
    ]
    scratch += [vmem((SIDE, CH, T0 * CH), bf16)] * (2 * SLOTS)
    scratch += [vmem((CH, T0 * CH), f32)] * SLOTS
    scratch += [vmem((2, 3, CH, T0 * CH // 2), bf16)] * (2 * SLOTS)
    scratch += [vmem((2, CH, T0 * CH // 2), f32)] * SLOTS
    scratch += [
        dma((CHUNKS, W)),
        dma,
        dma,
        dma,
        dma((CHUNKS, W, 2, 2)),
        dma((CHUNKS, W, 2, 2)),
        dma((CHUNKS, W, 2)),
        dma((CHUNKS, W, 2)),
        dma((CHUNKS, W, 2)),
        dma((CHUNKS, W, 2)),
        dma((CHUNKS, W, 2, 2)),
        dma((CHUNKS, W, 2, 2)),
        dma((SLOTS, SIDE)),
        dma((SLOTS, SIDE)),
        dma((SLOTS, 2, 3)),
        dma((SLOTS, 2, 3)),
    ]
    smem = pl.BlockSpec(memory_space=pltpu.SMEM)
    hbm = pl.BlockSpec(memory_space=pl.ANY)
    return pl.pallas_call(
        kernel,
        out_shape=jax.ShapeDtypeStruct((SLOTS, T0, CH, CH), f32),
        in_specs=[smem, smem, hbm, hbm, hbm, hbm],
        out_specs=pl.BlockSpec(memory_space=pltpu.VMEM),
        scratch_shapes=scratch,
        compiler_params=pltpu.CompilerParams(
            collective_id=0, has_side_effects=True, vmem_limit_bytes=67043328
        ),
        name="correlate",
    )(requests.T, pairs.transpose(0, 2, 1), counts, spectra, tables, turns)


def solution(mesh):
    placed = (P("tiles", None, None, None, "lag"), P(), P("tiles", None, None), P("tiles"), P(), P())
    tables, turns = phase_tables()
    mapped = jax.shard_map(
        per_device,
        mesh=mesh,
        in_specs=placed,
        out_specs=P("tiles", "lag", None, None),
        check_vma=False,
    )

    def run(spectra, requests, pairs, counts):
        return mapped(spectra, requests, pairs, counts, jnp.asarray(tables), jnp.asarray(turns))

    return run
```

```python
import functools
import math

import jax
import jax.numpy as jnp
import numpy as np
from jax import lax
from jax.experimental import pallas as pl
from jax.experimental.pallas import tpu as pltpu
from jax.sharding import PartitionSpec as P

MESH = pl.DeviceIdType.MESH
F = 8192
W = 2
LAGS = 64
CH = 128
BAND = 1024
NEED = 6
SLOTS = 3
SIDE = 4
T1 = 8
T0 = 8
WIDTHS = (256, 256, 256, 128, 128)
STARTS = (0, 256, 512, 768, 896)
CHUNKS = len(WIDTHS)
LAST = CHUNKS - 1
BUFFER = (0, 1, 0, 2, 3)
BUFFER_WIDTHS = (256, 256, 128, 128)
BUFFERS = len(BUFFER_WIDTHS)
ENTRIES = {True: 5, False: 6}
EARLY = (0, 3, 3, 3, 2)
NORM = 1.0 / math.sqrt(2.0 * W * F)


COARSE = T0 * np.arange(T1) - LAGS // 2
FINE = -np.arange(T0)


def phase_tables():
    freqs = np.arange(BAND, dtype=np.int64)

    def table(shifts):
        angles = (freqs[None, :] * shifts[:, None] % F) * (2.0 * math.pi / F)
        return np.stack([np.cos(angles), np.sin(angles)], axis=1)

    base = np.stack([table(COARSE), table(FINE)]).astype(np.float32)
    bands = np.arange(F // BAND, dtype=np.int64)
    turns = (bands[:, None] * BAND * FINE[None, :] % F) * (2.0 * math.pi / F)
    turn = np.stack([np.cos(turns), np.sin(turns)], axis=-1).astype(np.float32)
    return base, np.repeat(turn[..., None], 128, axis=-1)


def pick(flags, values):
    total = jnp.int32(0)
    for flag, value in zip(flags, values, strict=True):
        total = total + jnp.where(flag, value, 0)
    return total


def where_lies(req_ref, node, q, along, by_y):
    block = req_ref[q, node]
    holder = lax.div(block, 2)
    hy, hz = lax.div(holder, SIDE), lax.rem(holder, SIDE)
    h_along, h_across = (hy, hz) if by_y else (hz, hy)
    return lax.rem(h_along - along + SIDE, SIDE), h_across, lax.rem(block, 2)


def node_of(along, across, by_y):
    return along * SIDE + across if by_y else across * SIDE + along


def request_plan(req_ref, along, across, by_y):
    rel, index = [], []
    for q in range(NEED):
        r, h_across, inside = where_lies(
            req_ref, node_of(along, across, by_y), q, along, by_y
        )
        rel.append(r)
        index.append(2 * lax.rem(h_across - across + SIDE, SIDE) + inside)
    rank = []
    for q in range(NEED):
        total = jnp.int32(0)
        for earlier in range(q):
            total = total + jnp.where(rel[earlier] == rel[q], 1, 0)
        rank.append(total)
    return rel, index, rank


def ring_plan(req_ref, across, by_y, tight):
    near, far, below = [], [], []
    for i in range(SIDE):
        rel = [
            where_lies(req_ref, node_of(i, across, by_y), q, i, by_y)[0] for q in range(NEED)
        ]
        for into, value in ((near, 1), (far, 2), (below, 3)):
            into.append(pick([r == value for r in rel], [1] * NEED))
    if not tight:
        plus = [jnp.minimum(jnp.minimum(f, 2), 4 - n) for n, f in zip(near, far, strict=True)]
        return near, far, below, plus, None

    def clamp(value, f):
        return jnp.minimum(jnp.maximum(value, jnp.maximum(f - 2, 0)), jnp.minimum(f, 2))

    def half(value):
        return lax.div(value + 16, 2) - 8

    def attempt(up, order):
        p = [clamp(half(below[i] - near[i] + far[i] + 1 - up), far[i]) for i in range(SIDE)]
        for i in order:
            j, k = (i + 1) % SIDE, (i - 1) % SIDE
            high = jnp.maximum(near[i] + p[k], near[j] + p[j])
            low = jnp.maximum(below[i] + far[j] - p[j], below[k] + far[k] - p[k])
            p[i] = clamp(half(low + far[i] - high + up), far[i])
        good = jnp.int32(1)
        for i in range(SIDE):
            j, k = (i + 1) % SIDE, (i - 1) % SIDE
            for final, passing in (
                (near[i] + p[i], p[k]),
                (below[i] + far[i] - p[i], far[j] - p[j]),
            ):
                fits = (final <= 3) & (passing <= 2) | (final == 4) & (passing <= 1)
                good = good * jnp.where(fits, 1, 0)
            good = good * jnp.where(far[i] - p[i] <= 2, 1, 0) * jnp.where(p[i] <= 2, 1, 0)
        return p, good

    first, good = attempt(1, (0, 1, 2, 3))
    second, also = attempt(0, (3, 2, 1, 0))
    plus = [jnp.where(good == 1, a, b) for a, b in zip(first, second, strict=True)]
    return near, far, below, plus, jnp.maximum(good, also)


def kernel(tight, *args):
    req_ref, pairs_ref, counts_hbm, x_hbm, tab_hbm, turn_hbm, o_ref = args[:7]
    fits_ref = args[7] if tight else None
    rest = list(args[8:] if tight else args[7:])
    entries = ENTRIES[tight]
    first_finals = slice(2, entries - 2), slice(entries - 2, entries)

    def take(count):
        taken, rest[:count] = rest[:count], []
        return taken

    R = [take(CHUNKS) for _ in range(W)]
    G = [take(CHUNKS) for _ in range(W)]
    GS = [take(BUFFERS) for _ in range(W)]
    tab, turn, u, v, acc, loc, counts_ref = take(7)
    PS, PR, S, XR, XS, YR = (take(SLOTS) for _ in range(6))
    local_sem, tab_sem, turn_sem, count_sem, s1, r1, s1b, r1b, sg, rg, sp, rp, sx, rx = take(14)

    me, lag = lax.axis_index("tiles"), lax.axis_index("lag")
    y, z = lax.div(me, SIDE), lax.rem(me, SIDE)
    x, core = lax.div(lag, 2), lax.rem(lag, 2)

    def shift(a, by):
        return lax.rem(a + by + SIDE, SIDE)

    def at(by_y, by):
        return (shift(y, by) * SIDE + z, lag) if by_y else (y * SIDE + shift(z, by), lag)

    def along_x(by):
        return (me, shift(x, by) * 2 + core)

    partner = (me, 2 * x + 1 - core)

    tables = pltpu.make_async_copy(tab_hbm, tab, tab_sem)
    turns = pltpu.make_async_copy(turn_hbm.at[lag], turn, turn_sem)
    loads = {}
    for c in range(CHUNKS):
        for w in range(W):
            loads[c, w] = pltpu.make_async_copy(
                x_hbm.at[:, w, :, :, pl.ds(STARTS[c], WIDTHS[c])], R[w][c].at[0:2], local_sem.at[c, w]
            )
            loads[c, w].start()
    tables.start()
    turns.start()
    live_count = pltpu.make_async_copy(counts_hbm, counts_ref, count_sem)
    live_count.start()
    barrier = pltpu.get_barrier_semaphore()
    friends = [at(True, -1), at(True, 1), at(False, -1), at(False, 1)]
    friends += [along_x(-1), along_x(1), partner]
    for friend in friends:
        pl.semaphore_signal(barrier, inc=1, device_id=friend, device_id_type=MESH)
    pl.semaphore_wait(barrier, len(friends))

    def remote(src, dst, send, recv, to):
        copy = pltpu.make_async_remote_copy(
            src_ref=src, dst_ref=dst, send_sem=send, recv_sem=recv, device_id=to, device_id_type=MESH
        )
        copy.start()
        return copy

    first, second, transit, final, arrival = {}, {}, {}, {}, {}

    def start_first(c):
        for w in range(W):
            loads[c, w].wait()
            for k, (by, slot) in enumerate(((-1, 1), (1, 3))):
                for b in (k, 1 - k):
                    first[c, w, k, b] = remote(
                        R[w][c].at[b],
                        R[w][c].at[2 * slot + b],
                        s1.at[c, w, k, b],
                        r1.at[c, w, k, b],
                        at(w == 1, by),
                    )

    def start_second(c):
        for w in range(W):
            for k, (by, slot) in enumerate(((-1, 1), (1, 3))):
                first[c, w, k, k].wait_recv()
                second[c, w, k] = remote(
                    R[w][c].at[2 * slot + k],
                    R[w][c].at[4 + k],
                    s1b.at[c, w, k],
                    r1b.at[c, w, k],
                    at(w == 1, by),
                )

    start_first(0)
    start_first(1)

    direct, passed_on, shared, coming = {}, {}, {}, {}
    for w in range(W):
        along, across = (y, z) if w == 0 else (z, y)
        by_y = w == 0
        near, far, below, plus, _ = ring_plan(req_ref, across, by_y, tight)

        def of(values, there):
            return pick([there == i for i in range(SIDE)], values)

        for k, (by, mine, count) in enumerate(((-1, 1, near), (1, 3, below))):
            there = shift(along, by)
            rel, index, rank = request_plan(req_ref, there, across, by_y)
            for j in range(4):
                direct[w, k, j] = pick(
                    [(a == mine) & (b == j) for a, b in zip(rel, rank, strict=True)], index
                )
            up = of(plus, there)
            coming[w, k] = up if k == 0 else of(far, there) - up
            shared[w, k] = of(count, there) + coming[w, k] == 4
        there = shift(along, 2)
        rel, index, rank = request_plan(req_ref, there, across, by_y)
        up = of(plus, there)
        for j in range(2):
            passed_on[w, 0, j] = pick(
                [(a == 2) & (b < up) & (b == j) for a, b in zip(rel, rank, strict=True)], index
            )
            passed_on[w, 1, j] = pick(
                [(a == 2) & (b - up == j) for a, b in zip(rel, rank, strict=True)], index
            )
        if tight:
            for k in range(2):
                n = coming[w, k]
                last_direct = jnp.where(
                    n == 0, direct[w, k, 3], jnp.where(n == 1, direct[w, k, 2], direct[w, k, 1])
                )
                passed_on[w, k, 1] = jnp.where(shared[w, k], last_direct, passed_on[w, k, 1])
        rel, index, rank = request_plan(req_ref, along, across, by_y)
        up = of(plus, along)
        for q in range(NEED):
            r = rank[q]
            entry = []
            for k, (count, n) in enumerate(((near, up), (below, of(far, along) - up))):
                total = of(count, along)
                e = 2 + r
                if tight:
                    e = jnp.where((total + n == 4) & (r == total - 1), 1, e)
                entry.append(8 + k * entries + e)
            two = jnp.where(
                r < up, 8 + entries - 1 - r, 8 + 2 * entries - 1 - (r - up)
            )
            found = jnp.where(rel[q] == 2, two, jnp.where(rel[q] == 3, entry[1], entry[0]))
            loc[w, q] = jnp.where(rel[q] == 0, index[q], found)
    if tight:
        good = jnp.int32(1)
        for w in range(W):
            good = lax.fori_loop(
                0,
                SIDE,
                lambda across, so_far, w=w: so_far * ring_plan(req_ref, across, w == 0, True)[4],
                good,
            )
        fits_ref[0] = good

    def start_third(c):
        if BUFFER[c] in BUFFER[:c]:
            before = BUFFER.index(BUFFER[c])
            for w in range(W):
                for k in range(2):
                    transit.pop((before, w, k)).wait_send()
                    final.pop((before, w, k, 0)).wait_send()
                    final.pop((before, w, k, 1)).wait_send()
        for w in range(W):
            for k in range(2):
                first[c, w, k, 1 - k].wait_recv()
                second[c, w, k].wait_recv()
        for w in range(W):
            for k in range(2):
                for j in range(2):
                    GS[w][BUFFER[c]][k * entries + j] = R[w][c][passed_on[w, k, j]]
        for w in range(W):
            for k in range(2):
                transit[c, w, k] = send_group(c, w, k, 0, slice(0, 2))
        for w in range(W):
            for k in range(2):
                for j in range(entries - 4):
                    GS[w][BUFFER[c]][k * entries + 2 + j] = R[w][c][direct[w, k, j]]
        for w in range(W):
            for k in range(2):
                final[c, w, k, 0] = send_group(c, w, k, 1, first_finals[0])
                arrival[c, w, k, 0] = final[c, w, k, 0]

    def send_group(c, w, k, group, which):
        rows = slice(k * entries + which.start, k * entries + which.stop)
        return remote(
            GS[w][BUFFER[c]].at[rows],
            G[w][c].at[rows],
            sg.at[c, w, k, group],
            rg.at[c, w, k, group],
            at(w == 0, (-1, 1)[k]),
        )

    def start_fourth(c):
        for w in range(W):
            for k in range(2):
                transit[c, w, k].wait_recv()
        for w in range(W):
            for k in range(2):
                for n in (1, 0):
                    e = entries - 1 - n
                    own = R[w][c][direct[w, k, e - 2]]
                    passing = G[w][c][k * entries + n]
                    GS[w][BUFFER[c]][k * entries + e] = jnp.where(
                        coming[w, k] > n, passing, own
                    )
        for w in range(W):
            for k in range(2):
                final[c, w, k, 1] = send_group(c, w, k, 2, first_finals[1])
                arrival[c, w, k, 1] = final[c, w, k, 1]

    def wait_finals(c):
        for w in range(W):
            for k in range(2):
                arrival[c, w, k, 0].wait_recv()
                arrival[c, w, k, 1].wait_recv()

    def turn_fine():
        for t in range(T0):
            cos, sin = tab[1, t, 0:1, :], tab[1, t, 1:2, :]
            c, m = turn[t, 0:1, 0:1], turn[t, 1:2, 0:1]
            tab[1, t, 0:1, :] = cos * c - sin * m
            tab[1, t, 1:2, :] = cos * m + sin * c

    STRIP = 32

    def compute(c, s):
        kc, first_col = WIDTHS[c], STARTS[c]
        cols = slice(first_col, first_col + kc)
        for w in range(W):
            for side, dst in enumerate((u, v)):
                where = loc[w, pairs_ref[0, side, s]]
                i = jnp.minimum(where, 7)
                g = jnp.minimum(jnp.maximum(where - 8, 0), 2 * entries - 1)

                def strip(r, carry, w=w, side=side, dst=dst, i=i, g=g, where=where):
                    rows = pl.ds(pl.multiple_of(r * STRIP, STRIP), STRIP)
                    block = jnp.where(
                        where < 8, R[w][c][i, :, rows, :], G[w][c][g, :, rows, :]
                    )
                    real, imag = block[0].astype(jnp.float32), block[1].astype(jnp.float32)
                    base = 2 * w * kc
                    for t in range(8):
                        cos = tab[side, t, 0:1, cols]
                        sin = tab[side, t, 1:2, cols]
                        out = pl.ds(pl.multiple_of(t * CH + r * STRIP, STRIP), STRIP)
                        dst[out, base : base + kc] = (real * cos - imag * sin).astype(jnp.bfloat16)
                        dst[out, base + kc : base + 2 * kc] = (real * sin + imag * cos).astype(
                            jnp.bfloat16
                        )
                    return carry

                if tight:
                    for r in range(CH // STRIP):
                        strip(r, 0)
                else:
                    lax.fori_loop(0, CH // STRIP, strip, 0)

        wide = T0 * CH if tight else 256

        def multiply(n, carry):
            span = pl.ds(pl.multiple_of(n * wide, wide), wide)
            part = lax.dot_general(
                u[:, : 4 * kc],
                v[span, : 4 * kc],
                (((1,), (1,)), ((), ())),
                preferred_element_type=jnp.float32,
            )
            if c == 0:
                acc[s, :, span] = part
            else:
                acc[s, :, span] += part
            return carry

        if tight:
            multiply(0, 0)
        else:
            lax.fori_loop(0, T0 * CH // wide, multiply, 0)

    def compute_some(c, slots, begin=0):
        def one(s, carry):
            compute(c, s)
            return carry

        lax.fori_loop(begin, slots, one, 0)

    pair_copy, x_copy = {}, {}
    ORDER = (2, 1, -1, 0)

    def rows_of(there, which):
        return pl.ds(pl.multiple_of((2 * there + which) * CH, CH), CH)

    def send_pair(s):
        for n, by in enumerate(ORDER):
            block = acc[s, rows_of(shift(x, by), 1 - core), :] * NORM
            PS[s][n] = block.astype(jnp.bfloat16)
            pair_copy[s, n] = remote(
                PS[s].at[n], PR[s].at[n], sp.at[s, n], rp.at[s, n], partner
            )

    HALF = T0 * CH // 2
    lo, hi = slice(0, HALF), slice(HALF, 2 * HALF)

    def chip_sum(s):
        def total(by):
            n = ORDER.index(by)
            pair_copy[s, n].wait_recv()
            mine = acc[s, rows_of(shift(x, by), core), :] * NORM
            return mine + PR[s][n].astype(jnp.float32)

        far = total(2).astype(jnp.bfloat16)
        XS[s][0, 0] = far[:, lo]
        XS[s][1, 0] = far[:, hi]
        for k, by in enumerate((1, -1)):
            x_copy[s, k, 0] = remote(
                XS[s].at[k, 0], XR[s].at[k, 0], sx.at[s, k, 0], rx.at[s, k, 0], along_x(by)
            )
        for k, by in enumerate((1, -1)):
            near = total(by)
            relayed, own = (lo, hi) if k == 0 else (hi, lo)
            YR[s][k] = near[:, relayed]
            XS[s][k, 1] = near[:, own].astype(jnp.bfloat16)
            x_copy[s, k, 1] = remote(
                XS[s].at[k, 1], XR[s].at[k, 1], sx.at[s, k, 1], rx.at[s, k, 1], along_x(by)
            )
        S[s][...] = total(0)

    def relay(s):
        for k, by in enumerate((1, -1)):
            x_copy[s, k, 0].wait_recv()
            XS[s][k, 2] = (YR[s][k] + XR[s][k, 0].astype(jnp.float32)).astype(jnp.bfloat16)
            x_copy[s, k, 2] = remote(
                XS[s].at[k, 2], XR[s].at[k, 2], sx.at[s, k, 2], rx.at[s, k, 2], along_x(by)
            )

    def finish(s):
        for k in range(2):
            x_copy[s, k, 1].wait_recv()
            x_copy[s, k, 2].wait_recv()
        low = S[s][:, lo] + XR[s][0, 2].astype(jnp.float32) + XR[s][1, 1].astype(jnp.float32)
        high = S[s][:, hi] + XR[s][0, 1].astype(jnp.float32) + XR[s][1, 2].astype(jnp.float32)
        live = s < counts_ref[0]
        for t in range(T0 // 2):
            o_ref[s, t] = jnp.where(live, low[:, t * CH : (t + 1) * CH], 0.0)
            o_ref[s, T0 // 2 + t] = jnp.where(live, high[:, t * CH : (t + 1) * CH], 0.0)

    tables.wait()
    turns.wait()
    turn_fine()
    live_count.wait()
    start_second(0)
    start_first(2)
    for c in range(CHUNKS):
        start_third(c)
        if c > 0:
            wait_finals(c - 1)
            compute_some(c - 1, EARLY[c])
        start_fourth(c)
        if c + 1 < CHUNKS:
            start_second(c + 1)
        if c + 3 < CHUNKS:
            start_first(c + 3)
        if c > 0:
            for n in range(EARLY[c], SLOTS):
                compute(c - 1, n)
    last = LAST
    wait_finals(last)
    compute(last, 0)
    send_pair(0)
    compute(last, 1)
    send_pair(1)
    chip_sum(0)
    compute(last, 2)
    send_pair(2)
    relay(0)
    chip_sum(1)
    relay(1)
    chip_sum(2)
    finish(0)
    relay(2)
    finish(1)
    finish(2)

    for copy in list(first.values()) + list(second.values()):
        copy.wait_send()
    for copy in list(transit.values()) + list(final.values()):
        copy.wait_send()
    for copy in list(pair_copy.values()) + list(x_copy.values()):
        copy.wait_send()


def correlate(tight, spectra, requests, pairs, counts, tables, turns):
    entries = ENTRIES[tight]
    bf16, f32 = jnp.bfloat16, jnp.float32
    vmem, dma = pltpu.VMEM, pltpu.SemaphoreType.DMA
    scratch = []
    for lead in (8, 2 * entries):
        scratch += [vmem((lead, 2, CH, width), bf16) for width in WIDTHS] * W
    scratch += [vmem((2 * entries, 2, CH, width), bf16) for width in BUFFER_WIDTHS] * W
    scratch += [
        vmem((2, 8, 2, BAND), f32),
        vmem((8, 2, 128), f32),
        vmem((T1 * CH, 2 * W * max(WIDTHS)), bf16),
        vmem((T0 * CH, 2 * W * max(WIDTHS)), bf16),
        vmem((SLOTS, T1 * CH, T0 * CH), f32),
        pltpu.SMEM((W, NEED), jnp.int32),
        pltpu.SMEM((1,), jnp.int32),
    ]
    scratch += [vmem((SIDE, CH, T0 * CH), bf16)] * (2 * SLOTS)
    scratch += [vmem((CH, T0 * CH), f32)] * SLOTS
    scratch += [vmem((2, 3, CH, T0 * CH // 2), bf16)] * (2 * SLOTS)
    scratch += [vmem((2, CH, T0 * CH // 2), f32)] * SLOTS
    scratch += [
        dma((CHUNKS, W)),
        dma,
        dma,
        dma,
        dma((CHUNKS, W, 2, 2)),
        dma((CHUNKS, W, 2, 2)),
        dma((CHUNKS, W, 2)),
        dma((CHUNKS, W, 2)),
        dma((CHUNKS, W, 2, 3)),
        dma((CHUNKS, W, 2, 3)),
        dma((SLOTS, SIDE)),
        dma((SLOTS, SIDE)),
        dma((SLOTS, 2, 3)),
        dma((SLOTS, 2, 3)),
    ]
    smem = pl.BlockSpec(memory_space=pltpu.SMEM)
    hbm = pl.BlockSpec(memory_space=pl.ANY)
    out_shape = [jax.ShapeDtypeStruct((SLOTS, T0, CH, CH), f32)]
    out_specs = [pl.BlockSpec(memory_space=pltpu.VMEM)]
    if tight:
        out_shape.append(jax.ShapeDtypeStruct((1,), jnp.int32))
        out_specs.append(smem)
    return pl.pallas_call(
        functools.partial(kernel, tight),
        out_shape=out_shape,
        in_specs=[smem, smem, hbm, hbm, hbm, hbm],
        out_specs=out_specs,
        scratch_shapes=scratch,
        compiler_params=pltpu.CompilerParams(
            collective_id=0 if tight else 1, has_side_effects=True, vmem_limit_bytes=67043328
        ),
        name="correlate_tight" if tight else "correlate_any",
    )(requests.T, pairs.transpose(0, 2, 1), counts, spectra, tables, turns)


def per_device(*operands):
    summed, fits = correlate(True, *operands)
    return lax.cond(fits[0] == 1, lambda: summed, lambda: correlate(False, *operands)[0])


def solution(mesh):
    placed = (P("tiles", None, None, None, "lag"), P(), P("tiles", None, None), P("tiles"), P(), P())
    tables, turns = phase_tables()
    mapped = jax.shard_map(
        per_device,
        mesh=mesh,
        in_specs=placed,
        out_specs=P("tiles", "lag", None, None),
        check_vma=False,
    )

    def run(spectra, requests, pairs, counts):
        return mapped(spectra, requests, pairs, counts, jnp.asarray(tables), jnp.asarray(turns))

    return run
```

```python
import functools
import math

import jax
import jax.numpy as jnp
import numpy as np
from jax import lax
from jax.experimental import pallas as pl
from jax.experimental.pallas import tpu as pltpu
from jax.sharding import PartitionSpec as P

MESH = pl.DeviceIdType.MESH
F = 8192
W = 2
LAGS = 64
CH = 128
BAND = 1024
NEED = 6
SLOTS = 3
SIDE = 4
T1 = 8
T0 = 8
WIDTHS = (256, 256, 256, 256)
STARTS = (0, 256, 512, 768)
CHUNKS = len(WIDTHS)
LAST = CHUNKS - 1
BUFFER = (0, 1, 0, 1)
BUFFER_WIDTHS = (256, 256)
BUFFERS = len(BUFFER_WIDTHS)
ENTRIES = {True: 5, False: 6}
BEFORE_FOURTH = ((), ((0, 0, 3),), ((1, 0, 3),), ((2, 0, 2),))
AFTER_FOURTH = ((), (), (), ((2, 2, 3),))
NORM = 1.0 / math.sqrt(2.0 * W * F)


COARSE = T0 * np.arange(T1) - LAGS // 2
FINE = -np.arange(T0)


def phase_tables():
    freqs = np.arange(BAND, dtype=np.int64)

    def table(shifts):
        angles = (freqs[None, :] * shifts[:, None] % F) * (2.0 * math.pi / F)
        return np.stack([np.cos(angles), np.sin(angles)], axis=1)

    base = np.stack([table(COARSE), table(FINE)]).astype(np.float32)
    bands = np.arange(F // BAND, dtype=np.int64)
    turns = (bands[:, None] * BAND * FINE[None, :] % F) * (2.0 * math.pi / F)
    turn = np.stack([np.cos(turns), np.sin(turns)], axis=-1).astype(np.float32)
    return base, np.repeat(turn[..., None], 128, axis=-1)


def pick(flags, values):
    total = jnp.int32(0)
    for flag, value in zip(flags, values, strict=True):
        total = total + jnp.where(flag, value, 0)
    return total


def where_lies(req_ref, node, q, along, by_y):
    block = req_ref[q, node]
    holder = lax.div(block, 2)
    hy, hz = lax.div(holder, SIDE), lax.rem(holder, SIDE)
    h_along, h_across = (hy, hz) if by_y else (hz, hy)
    return lax.rem(h_along - along + SIDE, SIDE), h_across, lax.rem(block, 2)


def node_of(along, across, by_y):
    return along * SIDE + across if by_y else across * SIDE + along


def request_plan(req_ref, along, across, by_y):
    rel, index = [], []
    for q in range(NEED):
        r, h_across, inside = where_lies(
            req_ref, node_of(along, across, by_y), q, along, by_y
        )
        rel.append(r)
        index.append(2 * lax.rem(h_across - across + SIDE, SIDE) + inside)
    rank = []
    for q in range(NEED):
        total = jnp.int32(0)
        for earlier in range(q):
            total = total + jnp.where(rel[earlier] == rel[q], 1, 0)
        rank.append(total)
    return rel, index, rank


def ring_plan(req_ref, across, by_y, tight):
    near, far, below = [], [], []
    for i in range(SIDE):
        rel = [
            where_lies(req_ref, node_of(i, across, by_y), q, i, by_y)[0] for q in range(NEED)
        ]
        for into, value in ((near, 1), (far, 2), (below, 3)):
            into.append(pick([r == value for r in rel], [1] * NEED))
    if not tight:
        plus = [jnp.minimum(jnp.minimum(f, 2), 4 - n) for n, f in zip(near, far, strict=True)]
        return near, far, below, plus, None

    def clamp(value, f):
        return jnp.minimum(jnp.maximum(value, jnp.maximum(f - 2, 0)), jnp.minimum(f, 2))

    def half(value):
        return lax.div(value + 16, 2) - 8

    def attempt(up, order):
        p = [clamp(half(below[i] - near[i] + far[i] + 1 - up), far[i]) for i in range(SIDE)]
        for i in order:
            j, k = (i + 1) % SIDE, (i - 1) % SIDE
            high = jnp.maximum(near[i] + p[k], near[j] + p[j])
            low = jnp.maximum(below[i] + far[j] - p[j], below[k] + far[k] - p[k])
            p[i] = clamp(half(low + far[i] - high + up), far[i])
        good = jnp.int32(1)
        for i in range(SIDE):
            j, k = (i + 1) % SIDE, (i - 1) % SIDE
            for final, passing in (
                (near[i] + p[i], p[k]),
                (below[i] + far[i] - p[i], far[j] - p[j]),
            ):
                fits = (final <= 3) & (passing <= 2) | (final == 4) & (passing <= 1)
                good = good * jnp.where(fits, 1, 0)
            good = good * jnp.where(far[i] - p[i] <= 2, 1, 0) * jnp.where(p[i] <= 2, 1, 0)
        return p, good

    first, good = attempt(1, (0, 1, 2, 3))
    second, also = attempt(0, (3, 2, 1, 0))
    plus = [jnp.where(good == 1, a, b) for a, b in zip(first, second, strict=True)]
    return near, far, below, plus, jnp.maximum(good, also)


def kernel(tight, *args):
    req_ref, pairs_ref, counts_hbm, x_hbm, tab_hbm, turn_hbm, o_ref = args[:7]
    fits_ref = args[7] if tight else None
    rest = list(args[8:] if tight else args[7:])
    entries = ENTRIES[tight]
    first_finals = slice(2, entries - 2), slice(entries - 2, entries)

    def take(count):
        taken, rest[:count] = rest[:count], []
        return taken

    R = [take(CHUNKS) for _ in range(W)]
    G = [take(CHUNKS) for _ in range(W)]
    GS = [take(BUFFERS) for _ in range(W)]
    tab, turn, u, v, acc, loc, counts_ref = take(7)
    PS, PR, S, XR, XS, YR = (take(SLOTS) for _ in range(6))
    local_sem, tab_sem, turn_sem, count_sem, s1, r1, s1b, r1b, sg, rg, sp, rp, sx, rx = take(14)

    me, lag = lax.axis_index("tiles"), lax.axis_index("lag")
    y, z = lax.div(me, SIDE), lax.rem(me, SIDE)
    x, core = lax.div(lag, 2), lax.rem(lag, 2)

    def shift(a, by):
        return lax.rem(a + by + SIDE, SIDE)

    def at(by_y, by):
        return (shift(y, by) * SIDE + z, lag) if by_y else (y * SIDE + shift(z, by), lag)

    def along_x(by):
        return (me, shift(x, by) * 2 + core)

    partner = (me, 2 * x + 1 - core)

    tables = pltpu.make_async_copy(tab_hbm, tab, tab_sem)
    turns = pltpu.make_async_copy(turn_hbm.at[lag], turn, turn_sem)
    loads = {}
    for c in range(CHUNKS):
        for w in range(W):
            loads[c, w] = pltpu.make_async_copy(
                x_hbm.at[:, w, :, :, pl.ds(STARTS[c], WIDTHS[c])], R[w][c].at[0:2], local_sem.at[c, w]
            )
            loads[c, w].start()
    tables.start()
    turns.start()
    live_count = pltpu.make_async_copy(counts_hbm, counts_ref, count_sem)
    live_count.start()
    barrier = pltpu.get_barrier_semaphore()
    friends = [at(True, -1), at(True, 1), at(False, -1), at(False, 1)]
    friends += [along_x(-1), along_x(1), partner]
    for friend in friends:
        pl.semaphore_signal(barrier, inc=1, device_id=friend, device_id_type=MESH)
    pl.semaphore_wait(barrier, len(friends))

    def remote(src, dst, send, recv, to):
        copy = pltpu.make_async_remote_copy(
            src_ref=src, dst_ref=dst, send_sem=send, recv_sem=recv, device_id=to, device_id_type=MESH
        )
        copy.start()
        return copy

    first, second, transit, final, arrival = {}, {}, {}, {}, {}

    def start_first(c):
        for w in range(W):
            loads[c, w].wait()
            for k, (by, slot) in enumerate(((-1, 1), (1, 3))):
                for b in (k, 1 - k):
                    first[c, w, k, b] = remote(
                        R[w][c].at[b],
                        R[w][c].at[2 * slot + b],
                        s1.at[c, w, k, b],
                        r1.at[c, w, k, b],
                        at(w == 1, by),
                    )

    def start_second(c):
        for w in range(W):
            for k, (by, slot) in enumerate(((-1, 1), (1, 3))):
                first[c, w, k, k].wait_recv()
                second[c, w, k] = remote(
                    R[w][c].at[2 * slot + k],
                    R[w][c].at[4 + k],
                    s1b.at[c, w, k],
                    r1b.at[c, w, k],
                    at(w == 1, by),
                )

    start_first(0)
    start_first(1)

    direct, passed_on, shared, coming = {}, {}, {}, {}
    for w in range(W):
        along, across = (y, z) if w == 0 else (z, y)
        by_y = w == 0
        near, far, below, plus, _ = ring_plan(req_ref, across, by_y, tight)

        def of(values, there):
            return pick([there == i for i in range(SIDE)], values)

        for k, (by, mine, count) in enumerate(((-1, 1, near), (1, 3, below))):
            there = shift(along, by)
            rel, index, rank = request_plan(req_ref, there, across, by_y)
            for j in range(4):
                direct[w, k, j] = pick(
                    [(a == mine) & (b == j) for a, b in zip(rel, rank, strict=True)], index
                )
            up = of(plus, there)
            coming[w, k] = up if k == 0 else of(far, there) - up
            shared[w, k] = of(count, there) + coming[w, k] == 4
        there = shift(along, 2)
        rel, index, rank = request_plan(req_ref, there, across, by_y)
        up = of(plus, there)
        for j in range(2):
            passed_on[w, 0, j] = pick(
                [(a == 2) & (b < up) & (b == j) for a, b in zip(rel, rank, strict=True)], index
            )
            passed_on[w, 1, j] = pick(
                [(a == 2) & (b - up == j) for a, b in zip(rel, rank, strict=True)], index
            )
        if tight:
            for k in range(2):
                n = coming[w, k]
                last_direct = jnp.where(
                    n == 0, direct[w, k, 3], jnp.where(n == 1, direct[w, k, 2], direct[w, k, 1])
                )
                passed_on[w, k, 1] = jnp.where(shared[w, k], last_direct, passed_on[w, k, 1])
        rel, index, rank = request_plan(req_ref, along, across, by_y)
        up = of(plus, along)
        for q in range(NEED):
            r = rank[q]
            entry = []
            for k, (count, n) in enumerate(((near, up), (below, of(far, along) - up))):
                total = of(count, along)
                e = 2 + r
                if tight:
                    e = jnp.where((total + n == 4) & (r == total - 1), 1, e)
                entry.append(8 + k * entries + e)
            two = jnp.where(
                r < up, 8 + entries - 1 - r, 8 + 2 * entries - 1 - (r - up)
            )
            found = jnp.where(rel[q] == 2, two, jnp.where(rel[q] == 3, entry[1], entry[0]))
            loc[w, q] = jnp.where(rel[q] == 0, index[q], found)
    if tight:
        good = jnp.int32(1)
        for w in range(W):
            good = lax.fori_loop(
                0,
                SIDE,
                lambda across, so_far, w=w: so_far * ring_plan(req_ref, across, w == 0, True)[4],
                good,
            )
        fits_ref[0] = good

    def start_third(c):
        if BUFFER[c] in BUFFER[:c]:
            before = BUFFER.index(BUFFER[c])
            for w in range(W):
                for k in range(2):
                    transit.pop((before, w, k)).wait_send()
                    final.pop((before, w, k, 0)).wait_send()
                    final.pop((before, w, k, 1)).wait_send()
        for w in range(W):
            for k in range(2):
                first[c, w, k, 1 - k].wait_recv()
                second[c, w, k].wait_recv()
        for w in range(W):
            for k in range(2):
                for j in range(2):
                    GS[w][BUFFER[c]][k * entries + j] = R[w][c][passed_on[w, k, j]]
        for w in range(W):
            for k in range(2):
                transit[c, w, k] = send_group(c, w, k, 0, slice(0, 2))
        for w in range(W):
            for k in range(2):
                for j in range(entries - 4):
                    GS[w][BUFFER[c]][k * entries + 2 + j] = R[w][c][direct[w, k, j]]
        for w in range(W):
            for k in range(2):
                final[c, w, k, 0] = send_group(c, w, k, 1, first_finals[0])
                arrival[c, w, k, 0] = final[c, w, k, 0]

    def send_group(c, w, k, group, which):
        rows = slice(k * entries + which.start, k * entries + which.stop)
        return remote(
            GS[w][BUFFER[c]].at[rows],
            G[w][c].at[rows],
            sg.at[c, w, k, group],
            rg.at[c, w, k, group],
            at(w == 0, (-1, 1)[k]),
        )

    def start_fourth(c):
        for w in range(W):
            for k in range(2):
                transit[c, w, k].wait_recv()
        for w in range(W):
            for k in range(2):
                for n in (1, 0):
                    e = entries - 1 - n
                    own = R[w][c][direct[w, k, e - 2]]
                    passing = G[w][c][k * entries + n]
                    GS[w][BUFFER[c]][k * entries + e] = jnp.where(
                        coming[w, k] > n, passing, own
                    )
        for w in range(W):
            for k in range(2):
                final[c, w, k, 1] = send_group(c, w, k, 2, first_finals[1])
                arrival[c, w, k, 1] = final[c, w, k, 1]

    def wait_finals(c):
        for w in range(W):
            for k in range(2):
                arrival[c, w, k, 0].wait_recv()
                arrival[c, w, k, 1].wait_recv()

    def turn_fine():
        for t in range(T0):
            cos, sin = tab[1, t, 0:1, :], tab[1, t, 1:2, :]
            c, m = turn[t, 0:1, 0:1], turn[t, 1:2, 0:1]
            tab[1, t, 0:1, :] = cos * c - sin * m
            tab[1, t, 1:2, :] = cos * m + sin * c

    STRIP = 32

    def compute(c, s):
        kc, first_col = WIDTHS[c], STARTS[c]
        cols = slice(first_col, first_col + kc)
        for w in range(W):
            for side, dst in enumerate((u, v)):
                where = loc[w, pairs_ref[0, side, s]]
                i = jnp.minimum(where, 7)
                g = jnp.minimum(jnp.maximum(where - 8, 0), 2 * entries - 1)

                def strip(r, carry, w=w, side=side, dst=dst, i=i, g=g, where=where):
                    rows = pl.ds(pl.multiple_of(r * STRIP, STRIP), STRIP)
                    block = jnp.where(
                        where < 8, R[w][c][i, :, rows, :], G[w][c][g, :, rows, :]
                    )
                    real, imag = block[0].astype(jnp.float32), block[1].astype(jnp.float32)
                    base = 2 * w * kc
                    for t in range(8):
                        cos = tab[side, t, 0:1, cols]
                        sin = tab[side, t, 1:2, cols]
                        out = pl.ds(pl.multiple_of(t * CH + r * STRIP, STRIP), STRIP)
                        dst[out, base : base + kc] = (real * cos - imag * sin).astype(jnp.bfloat16)
                        dst[out, base + kc : base + 2 * kc] = (real * sin + imag * cos).astype(
                            jnp.bfloat16
                        )
                    return carry

                if tight:
                    for r in range(CH // STRIP):
                        strip(r, 0)
                else:
                    lax.fori_loop(0, CH // STRIP, strip, 0)

        wide = T0 * CH if tight else 256

        def multiply(n, carry):
            span = pl.ds(pl.multiple_of(n * wide, wide), wide)
            part = lax.dot_general(
                u[:, : 4 * kc],
                v[span, : 4 * kc],
                (((1,), (1,)), ((), ())),
                preferred_element_type=jnp.float32,
            )
            if c == 0:
                acc[s, :, span] = part
            else:
                acc[s, :, span] += part
            return carry

        if tight:
            multiply(0, 0)
        else:
            lax.fori_loop(0, T0 * CH // wide, multiply, 0)

    def compute_some(c, begin, end):
        if begin == 0:
            wait_finals(c)
        if end - begin == 1:
            compute(c, begin)
            return

        def one(s, carry):
            compute(c, s)
            return carry

        lax.fori_loop(begin, end, one, 0)

    pair_copy, x_copy = {}, {}
    ORDER = (2, 1, -1, 0)

    def rows_of(there, which):
        return pl.ds(pl.multiple_of((2 * there + which) * CH, CH), CH)

    def send_pair(s):
        for n, by in enumerate(ORDER):
            block = acc[s, rows_of(shift(x, by), 1 - core), :] * NORM
            PS[s][n] = block.astype(jnp.bfloat16)
            pair_copy[s, n] = remote(
                PS[s].at[n], PR[s].at[n], sp.at[s, n], rp.at[s, n], partner
            )

    HALF = T0 * CH // 2
    lo, hi = slice(0, HALF), slice(HALF, 2 * HALF)

    def chip_sum(s):
        def total(by):
            n = ORDER.index(by)
            pair_copy[s, n].wait_recv()
            mine = acc[s, rows_of(shift(x, by), core), :] * NORM
            return mine + PR[s][n].astype(jnp.float32)

        far = total(2).astype(jnp.bfloat16)
        XS[s][0, 0] = far[:, lo]
        XS[s][1, 0] = far[:, hi]
        for k, by in enumerate((1, -1)):
            x_copy[s, k, 0] = remote(
                XS[s].at[k, 0], XR[s].at[k, 0], sx.at[s, k, 0], rx.at[s, k, 0], along_x(by)
            )
        for k, by in enumerate((1, -1)):
            near = total(by)
            relayed, own = (lo, hi) if k == 0 else (hi, lo)
            YR[s][k] = near[:, relayed]
            XS[s][k, 1] = near[:, own].astype(jnp.bfloat16)
            x_copy[s, k, 1] = remote(
                XS[s].at[k, 1], XR[s].at[k, 1], sx.at[s, k, 1], rx.at[s, k, 1], along_x(by)
            )
        S[s][...] = total(0)

    def relay(s):
        for k, by in enumerate((1, -1)):
            x_copy[s, k, 0].wait_recv()
            XS[s][k, 2] = (YR[s][k] + XR[s][k, 0].astype(jnp.float32)).astype(jnp.bfloat16)
            x_copy[s, k, 2] = remote(
                XS[s].at[k, 2], XR[s].at[k, 2], sx.at[s, k, 2], rx.at[s, k, 2], along_x(by)
            )

    def finish(s):
        for k in range(2):
            x_copy[s, k, 1].wait_recv()
            x_copy[s, k, 2].wait_recv()
        low = S[s][:, lo] + XR[s][0, 2].astype(jnp.float32) + XR[s][1, 1].astype(jnp.float32)
        high = S[s][:, hi] + XR[s][0, 1].astype(jnp.float32) + XR[s][1, 2].astype(jnp.float32)
        live = s < counts_ref[0]
        for t in range(T0 // 2):
            span = slice(t * CH, (t + 1) * CH)
            o_ref[s, t] = jnp.where(live, low[:, span], 0.0).astype(jnp.bfloat16)
            o_ref[s, T0 // 2 + t] = jnp.where(live, high[:, span], 0.0).astype(jnp.bfloat16)

    tables.wait()
    turns.wait()
    turn_fine()
    live_count.wait()
    start_second(0)
    start_first(2)
    for c in range(CHUNKS):
        start_third(c)
        if c + 1 < CHUNKS:
            start_second(c + 1)
        if c + 3 < CHUNKS:
            start_first(c + 3)
        for chunk, begin, end in BEFORE_FOURTH[c]:
            compute_some(chunk, begin, end)
        start_fourth(c)
        for chunk, begin, end in AFTER_FOURTH[c]:
            compute_some(chunk, begin, end)
    last = LAST
    wait_finals(last)
    compute(last, 0)
    send_pair(0)
    chip_sum(0)
    compute(last, 1)
    send_pair(1)
    compute(last, 2)
    send_pair(2)
    relay(0)
    chip_sum(1)
    chip_sum(2)
    relay(1)
    finish(0)
    relay(2)
    finish(1)
    finish(2)

    for copy in list(first.values()) + list(second.values()):
        copy.wait_send()
    for copy in list(transit.values()) + list(final.values()):
        copy.wait_send()
    for copy in list(pair_copy.values()) + list(x_copy.values()):
        copy.wait_send()


def correlate(tight, spectra, requests, pairs, counts, tables, turns):
    entries = ENTRIES[tight]
    bf16, f32 = jnp.bfloat16, jnp.float32
    vmem, dma = pltpu.VMEM, pltpu.SemaphoreType.DMA
    scratch = []
    for lead in (8, 2 * entries):
        scratch += [vmem((lead, 2, CH, width), bf16) for width in WIDTHS] * W
    scratch += [vmem((2 * entries, 2, CH, width), bf16) for width in BUFFER_WIDTHS] * W
    scratch += [
        vmem((2, 8, 2, BAND), f32),
        vmem((8, 2, 128), f32),
        vmem((T1 * CH, 2 * W * max(WIDTHS)), bf16),
        vmem((T0 * CH, 2 * W * max(WIDTHS)), bf16),
        vmem((SLOTS, T1 * CH, T0 * CH), f32),
        pltpu.SMEM((W, NEED), jnp.int32),
        pltpu.SMEM((1,), jnp.int32),
    ]
    scratch += [vmem((SIDE, CH, T0 * CH), bf16)] * (2 * SLOTS)
    scratch += [vmem((CH, T0 * CH), f32)] * SLOTS
    scratch += [vmem((2, 3, CH, T0 * CH // 2), bf16)] * (2 * SLOTS)
    scratch += [vmem((2, CH, T0 * CH // 2), f32)] * SLOTS
    scratch += [
        dma((CHUNKS, W)),
        dma,
        dma,
        dma,
        dma((CHUNKS, W, 2, 2)),
        dma((CHUNKS, W, 2, 2)),
        dma((CHUNKS, W, 2)),
        dma((CHUNKS, W, 2)),
        dma((CHUNKS, W, 2, 3)),
        dma((CHUNKS, W, 2, 3)),
        dma((SLOTS, SIDE)),
        dma((SLOTS, SIDE)),
        dma((SLOTS, 2, 3)),
        dma((SLOTS, 2, 3)),
    ]
    smem = pl.BlockSpec(memory_space=pltpu.SMEM)
    hbm = pl.BlockSpec(memory_space=pl.ANY)
    out_shape = [jax.ShapeDtypeStruct((SLOTS, T0, CH, CH), bf16)]
    out_specs = [pl.BlockSpec(memory_space=pltpu.VMEM)]
    if tight:
        out_shape.append(jax.ShapeDtypeStruct((1,), jnp.int32))
        out_specs.append(smem)
    return pl.pallas_call(
        functools.partial(kernel, tight),
        out_shape=out_shape,
        in_specs=[smem, smem, hbm, hbm, hbm, hbm],
        out_specs=out_specs,
        scratch_shapes=scratch,
        compiler_params=pltpu.CompilerParams(
            collective_id=0 if tight else 1, has_side_effects=True, vmem_limit_bytes=67043328
        ),
        name="correlate_tight" if tight else "correlate_any",
    )(requests.T, pairs.transpose(0, 2, 1), counts, spectra, tables, turns)


def per_device(*operands):
    summed, fits = correlate(True, *operands)
    chosen = lax.cond(fits[0] == 1, lambda: summed, lambda: correlate(False, *operands)[0])
    return chosen.astype(jnp.float32)


def solution(mesh):
    placed = (P("tiles", None, None, None, "lag"), P(), P("tiles", None, None), P("tiles"), P(), P())
    tables, turns = phase_tables()
    mapped = jax.shard_map(
        per_device,
        mesh=mesh,
        in_specs=placed,
        out_specs=P("tiles", "lag", None, None),
        check_vma=False,
    )

    def run(spectra, requests, pairs, counts):
        return mapped(spectra, requests, pairs, counts, jnp.asarray(tables), jnp.asarray(turns))

    return run
```

```python
import functools
import math

import jax
import jax.numpy as jnp
import numpy as np
from jax import lax
from jax.experimental import pallas as pl
from jax.experimental.pallas import tpu as pltpu
from jax.sharding import PartitionSpec as P

MESH = pl.DeviceIdType.MESH
F = 8192
W = 2
LAGS = 64
CH = 128
BAND = 1024
NEED = 6
SLOTS = 3
SIDE = 4
T1 = 8
T0 = 8
WIDTHS = (256, 256, 256, 256)
STARTS = (0, 256, 512, 768)
CHUNKS = len(WIDTHS)
LAST = CHUNKS - 1
BUFFER = (0, 1, 0, 1)
BUFFER_WIDTHS = (256, 256)
BUFFERS = len(BUFFER_WIDTHS)
ENTRIES = {True: 5, False: 6}
BEFORE_FOURTH = ((), ((0, 0, 3),), ((1, 0, 3),), ((2, 0, 2),))
AFTER_FOURTH = ((), (), (), ((2, 2, 3),))
NORM = 1.0 / math.sqrt(2.0 * W * F)


COARSE = T0 * np.arange(T1) - LAGS // 2
FINE = -np.arange(T0)


def phase_tables():
    freqs = np.arange(BAND, dtype=np.int64)

    def table(shifts):
        angles = (freqs[None, :] * shifts[:, None] % F) * (2.0 * math.pi / F)
        return np.stack([np.cos(angles), np.sin(angles)], axis=1)

    base = np.stack([table(COARSE), table(FINE)]).astype(np.float32)
    bands = np.arange(F // BAND, dtype=np.int64)
    turns = (bands[:, None] * BAND * FINE[None, :] % F) * (2.0 * math.pi / F)
    turn = np.stack([np.cos(turns), np.sin(turns)], axis=-1).astype(np.float32)
    return base, np.repeat(turn[..., None], 128, axis=-1)


def pick(flags, values):
    total = jnp.int32(0)
    for flag, value in zip(flags, values, strict=True):
        total = total + jnp.where(flag, value, 0)
    return total


def where_lies(req_ref, node, q, along, by_y):
    block = req_ref[q, node]
    holder = lax.div(block, 2)
    hy, hz = lax.div(holder, SIDE), lax.rem(holder, SIDE)
    h_along, h_across = (hy, hz) if by_y else (hz, hy)
    return lax.rem(h_along - along + SIDE, SIDE), h_across, lax.rem(block, 2)


def node_of(along, across, by_y):
    return along * SIDE + across if by_y else across * SIDE + along


def request_plan(req_ref, along, across, by_y):
    rel, index = [], []
    for q in range(NEED):
        r, h_across, inside = where_lies(
            req_ref, node_of(along, across, by_y), q, along, by_y
        )
        rel.append(r)
        index.append(2 * lax.rem(h_across - across + SIDE, SIDE) + inside)
    rank = []
    for q in range(NEED):
        total = jnp.int32(0)
        for earlier in range(q):
            total = total + jnp.where(rel[earlier] == rel[q], 1, 0)
        rank.append(total)
    return rel, index, rank


def ring_plan(req_ref, across, by_y, tight):
    near, far, below = [], [], []
    for i in range(SIDE):
        rel = [
            where_lies(req_ref, node_of(i, across, by_y), q, i, by_y)[0] for q in range(NEED)
        ]
        for into, value in ((near, 1), (far, 2), (below, 3)):
            into.append(pick([r == value for r in rel], [1] * NEED))
    if not tight:
        plus = [jnp.minimum(jnp.minimum(f, 2), 4 - n) for n, f in zip(near, far, strict=True)]
        return near, far, below, plus, None

    def clamp(value, f):
        return jnp.minimum(jnp.maximum(value, jnp.maximum(f - 2, 0)), jnp.minimum(f, 2))

    def half(value):
        return lax.div(value + 16, 2) - 8

    def attempt(up, order):
        p = [clamp(half(below[i] - near[i] + far[i] + 1 - up), far[i]) for i in range(SIDE)]
        for i in order:
            j, k = (i + 1) % SIDE, (i - 1) % SIDE
            high = jnp.maximum(near[i] + p[k], near[j] + p[j])
            low = jnp.maximum(below[i] + far[j] - p[j], below[k] + far[k] - p[k])
            p[i] = clamp(half(low + far[i] - high + up), far[i])
        good = jnp.int32(1)
        for i in range(SIDE):
            j, k = (i + 1) % SIDE, (i - 1) % SIDE
            for final, passing in (
                (near[i] + p[i], p[k]),
                (below[i] + far[i] - p[i], far[j] - p[j]),
            ):
                fits = (final <= 3) & (passing <= 2) | (final == 4) & (passing <= 1)
                good = good * jnp.where(fits, 1, 0)
            good = good * jnp.where(far[i] - p[i] <= 2, 1, 0) * jnp.where(p[i] <= 2, 1, 0)
        return p, good

    first, good = attempt(1, (0, 1, 2, 3))
    second, also = attempt(0, (3, 2, 1, 0))
    plus = [jnp.where(good == 1, a, b) for a, b in zip(first, second, strict=True)]
    return near, far, below, plus, jnp.maximum(good, also)


def kernel(tight, *args):
    req_ref, pairs_ref, counts_hbm, x_hbm, tab_hbm, turn_hbm, o_ref = args[:7]
    fits_ref = args[7] if tight else None
    rest = list(args[8:] if tight else args[7:])
    entries = ENTRIES[tight]
    first_finals = slice(2, entries - 2), slice(entries - 2, entries)

    def take(count):
        taken, rest[:count] = rest[:count], []
        return taken

    R = [take(CHUNKS) for _ in range(W)]
    G = [take(CHUNKS) for _ in range(W)]
    GS = [take(BUFFERS) for _ in range(W)]
    tab, turn, u, v, acc, loc, counts_ref = take(7)
    PS, PR, S, XR, XS, YR = (take(SLOTS) for _ in range(6))
    local_sem, tab_sem, turn_sem, count_sem, s1, r1, s1b, r1b, sg, rg, sp, rp, sx, rx = take(14)

    me, lag = lax.axis_index("tiles"), lax.axis_index("lag")
    y, z = lax.div(me, SIDE), lax.rem(me, SIDE)
    x, core = lax.div(lag, 2), lax.rem(lag, 2)

    def shift(a, by):
        return lax.rem(a + by + SIDE, SIDE)

    def at(by_y, by):
        return (shift(y, by) * SIDE + z, lag) if by_y else (y * SIDE + shift(z, by), lag)

    def along_x(by):
        return (me, shift(x, by) * 2 + core)

    partner = (me, 2 * x + 1 - core)

    barrier = pltpu.get_barrier_semaphore()
    friends = [at(True, -1), at(True, 1), at(False, -1), at(False, 1)]
    friends += [along_x(-1), along_x(1), partner]
    for friend in friends:
        pl.semaphore_signal(barrier, inc=1, device_id=friend, device_id_type=MESH)
    tables = pltpu.make_async_copy(tab_hbm, tab, tab_sem)
    turns = pltpu.make_async_copy(turn_hbm.at[lag], turn, turn_sem)
    loads = {}
    for c in range(CHUNKS):
        for w in range(W):
            loads[c, w] = pltpu.make_async_copy(
                x_hbm.at[:, w, :, :, pl.ds(STARTS[c], WIDTHS[c])], R[w][c].at[0:2], local_sem.at[c, w]
            )
            loads[c, w].start()
    tables.start()
    turns.start()
    live_count = pltpu.make_async_copy(counts_hbm, counts_ref, count_sem)
    live_count.start()
    pl.semaphore_wait(barrier, len(friends))

    def remote(src, dst, send, recv, to):
        copy = pltpu.make_async_remote_copy(
            src_ref=src, dst_ref=dst, send_sem=send, recv_sem=recv, device_id=to, device_id_type=MESH
        )
        copy.start()
        return copy

    first, second, transit, final, arrival = {}, {}, {}, {}, {}

    def start_first(c):
        for w in range(W):
            loads[c, w].wait()
            for k, (by, slot) in enumerate(((-1, 1), (1, 3))):
                for b in (k, 1 - k):
                    first[c, w, k, b] = remote(
                        R[w][c].at[b],
                        R[w][c].at[2 * slot + b],
                        s1.at[c, w, k, b],
                        r1.at[c, w, k, b],
                        at(w == 1, by),
                    )

    def start_second(c):
        for w in range(W):
            for k, (by, slot) in enumerate(((-1, 1), (1, 3))):
                first[c, w, k, k].wait_recv()
                second[c, w, k] = remote(
                    R[w][c].at[2 * slot + k],
                    R[w][c].at[4 + k],
                    s1b.at[c, w, k],
                    r1b.at[c, w, k],
                    at(w == 1, by),
                )

    start_first(0)
    start_first(1)

    direct, passed_on, shared, coming = {}, {}, {}, {}
    for w in range(W):
        along, across = (y, z) if w == 0 else (z, y)
        by_y = w == 0
        near, far, below, plus, _ = ring_plan(req_ref, across, by_y, tight)

        def of(values, there):
            return pick([there == i for i in range(SIDE)], values)

        for k, (by, mine, count) in enumerate(((-1, 1, near), (1, 3, below))):
            there = shift(along, by)
            rel, index, rank = request_plan(req_ref, there, across, by_y)
            for j in range(4):
                direct[w, k, j] = pick(
                    [(a == mine) & (b == j) for a, b in zip(rel, rank, strict=True)], index
                )
            up = of(plus, there)
            coming[w, k] = up if k == 0 else of(far, there) - up
            shared[w, k] = of(count, there) + coming[w, k] == 4
        there = shift(along, 2)
        rel, index, rank = request_plan(req_ref, there, across, by_y)
        up = of(plus, there)
        for j in range(2):
            passed_on[w, 0, j] = pick(
                [(a == 2) & (b < up) & (b == j) for a, b in zip(rel, rank, strict=True)], index
            )
            passed_on[w, 1, j] = pick(
                [(a == 2) & (b - up == j) for a, b in zip(rel, rank, strict=True)], index
            )
        if tight:
            for k in range(2):
                n = coming[w, k]
                last_direct = jnp.where(
                    n == 0, direct[w, k, 3], jnp.where(n == 1, direct[w, k, 2], direct[w, k, 1])
                )
                passed_on[w, k, 1] = jnp.where(shared[w, k], last_direct, passed_on[w, k, 1])
        rel, index, rank = request_plan(req_ref, along, across, by_y)
        up = of(plus, along)
        for q in range(NEED):
            r = rank[q]
            entry = []
            for k, (count, n) in enumerate(((near, up), (below, of(far, along) - up))):
                total = of(count, along)
                e = 2 + r
                if tight:
                    e = jnp.where((total + n == 4) & (r == total - 1), 1, e)
                entry.append(8 + k * entries + e)
            two = jnp.where(
                r < up, 8 + entries - 1 - r, 8 + 2 * entries - 1 - (r - up)
            )
            found = jnp.where(rel[q] == 2, two, jnp.where(rel[q] == 3, entry[1], entry[0]))
            loc[w, q] = jnp.where(rel[q] == 0, index[q], found)
    if tight:
        good = jnp.int32(1)
        for w in range(W):
            good = lax.fori_loop(
                0,
                SIDE,
                lambda across, so_far, w=w: so_far * ring_plan(req_ref, across, w == 0, True)[4],
                good,
            )
        fits_ref[0] = good

    def start_third(c):
        if BUFFER[c] in BUFFER[:c]:
            before = BUFFER.index(BUFFER[c])
            for w in range(W):
                for k in range(2):
                    transit.pop((before, w, k)).wait_send()
                    final.pop((before, w, k, 0)).wait_send()
                    final.pop((before, w, k, 1)).wait_send()
        for w in range(W):
            for k in range(2):
                first[c, w, k, 1 - k].wait_recv()
                second[c, w, k].wait_recv()
        for w in range(W):
            for k in range(2):
                for j in range(2):
                    GS[w][BUFFER[c]][k * entries + j] = R[w][c][passed_on[w, k, j]]
        for w in range(W):
            for k in range(2):
                transit[c, w, k] = send_group(c, w, k, 0, slice(0, 2))
        for w in range(W):
            for k in range(2):
                for j in range(entries - 4):
                    GS[w][BUFFER[c]][k * entries + 2 + j] = R[w][c][direct[w, k, j]]
        for w in range(W):
            for k in range(2):
                final[c, w, k, 0] = send_group(c, w, k, 1, first_finals[0])
                arrival[c, w, k, 0] = final[c, w, k, 0]

    def send_group(c, w, k, group, which):
        rows = slice(k * entries + which.start, k * entries + which.stop)
        return remote(
            GS[w][BUFFER[c]].at[rows],
            G[w][c].at[rows],
            sg.at[c, w, k, group],
            rg.at[c, w, k, group],
            at(w == 0, (-1, 1)[k]),
        )

    def start_fourth(c):
        for w in range(W):
            for k in range(2):
                transit[c, w, k].wait_recv()
        for w in range(W):
            for k in range(2):
                for n in (1, 0):
                    e = entries - 1 - n
                    own = R[w][c][direct[w, k, e - 2]]
                    passing = G[w][c][k * entries + n]
                    GS[w][BUFFER[c]][k * entries + e] = jnp.where(
                        coming[w, k] > n, passing, own
                    )
        for w in range(W):
            for k in range(2):
                final[c, w, k, 1] = send_group(c, w, k, 2, first_finals[1])
                arrival[c, w, k, 1] = final[c, w, k, 1]

    def wait_finals(c):
        for w in range(W):
            for k in range(2):
                arrival[c, w, k, 0].wait_recv()
                arrival[c, w, k, 1].wait_recv()

    def turn_fine():
        for t in range(T0):
            cos, sin = tab[1, t, 0:1, :], tab[1, t, 1:2, :]
            c, m = turn[t, 0:1, 0:1], turn[t, 1:2, 0:1]
            tab[1, t, 0:1, :] = cos * c - sin * m
            tab[1, t, 1:2, :] = cos * m + sin * c

    STRIP = 32

    def compute(c, s):
        kc, first_col = WIDTHS[c], STARTS[c]
        cols = slice(first_col, first_col + kc)
        for w in range(W):
            for side, dst in enumerate((u, v)):
                where = loc[w, pairs_ref[0, side, s]]
                i = jnp.minimum(where, 7)
                g = jnp.minimum(jnp.maximum(where - 8, 0), 2 * entries - 1)

                def strip(r, carry, w=w, side=side, dst=dst, i=i, g=g, where=where):
                    rows = pl.ds(pl.multiple_of(r * STRIP, STRIP), STRIP)
                    block = jnp.where(
                        where < 8, R[w][c][i, :, rows, :], G[w][c][g, :, rows, :]
                    )
                    real, imag = block[0].astype(jnp.float32), block[1].astype(jnp.float32)
                    base = 2 * w * kc
                    for t in range(8):
                        out = pl.ds(pl.multiple_of(t * CH + r * STRIP, STRIP), STRIP)
                        if (COARSE, FINE)[side][t] == 0:
                            dst[out, base : base + kc] = block[0]
                            dst[out, base + kc : base + 2 * kc] = block[1]
                            continue
                        cos = tab[side, t, 0:1, cols]
                        sin = tab[side, t, 1:2, cols]
                        dst[out, base : base + kc] = (real * cos - imag * sin).astype(jnp.bfloat16)
                        dst[out, base + kc : base + 2 * kc] = (real * sin + imag * cos).astype(
                            jnp.bfloat16
                        )
                    return carry

                if tight:
                    for r in range(CH // STRIP):
                        strip(r, 0)
                else:
                    lax.fori_loop(0, CH // STRIP, strip, 0)

        wide = T0 * CH if tight else 256

        def multiply(n, carry):
            span = pl.ds(pl.multiple_of(n * wide, wide), wide)
            part = lax.dot_general(
                u[:, : 4 * kc],
                v[span, : 4 * kc],
                (((1,), (1,)), ((), ())),
                preferred_element_type=jnp.float32,
            )
            if c == 0:
                acc[s, :, span] = part
            else:
                acc[s, :, span] += part
            return carry

        if tight:
            multiply(0, 0)
        else:
            lax.fori_loop(0, T0 * CH // wide, multiply, 0)

    def compute_some(c, begin, end):
        if begin == 0:
            wait_finals(c)
        if end - begin == 1:
            compute(c, begin)
            return

        def one(s, carry):
            compute(c, s)
            return carry

        lax.fori_loop(begin, end, one, 0)

    pair_copy, x_copy = {}, {}
    ORDER = (2, 1, -1, 0)

    def rows_of(there, which):
        return pl.ds(pl.multiple_of((2 * there + which) * CH, CH), CH)

    def send_pair(s):
        for n, by in enumerate(ORDER):
            block = acc[s, rows_of(shift(x, by), 1 - core), :] * NORM
            PS[s][n] = block.astype(jnp.bfloat16)
            pair_copy[s, n] = remote(
                PS[s].at[n], PR[s].at[n], sp.at[s, n], rp.at[s, n], partner
            )

    HALF = T0 * CH // 2
    lo, hi = slice(0, HALF), slice(HALF, 2 * HALF)

    def chip_sum(s):
        def total(by):
            n = ORDER.index(by)
            pair_copy[s, n].wait_recv()
            mine = acc[s, rows_of(shift(x, by), core), :] * NORM
            return mine + PR[s][n].astype(jnp.float32)

        far = total(2).astype(jnp.bfloat16)
        XS[s][0, 0] = far[:, lo]
        XS[s][1, 0] = far[:, hi]
        for k, by in enumerate((1, -1)):
            x_copy[s, k, 0] = remote(
                XS[s].at[k, 0], XR[s].at[k, 0], sx.at[s, k, 0], rx.at[s, k, 0], along_x(by)
            )
        for k, by in enumerate((1, -1)):
            near = total(by)
            relayed, own = (lo, hi) if k == 0 else (hi, lo)
            YR[s][k] = near[:, relayed]
            XS[s][k, 1] = near[:, own].astype(jnp.bfloat16)
            x_copy[s, k, 1] = remote(
                XS[s].at[k, 1], XR[s].at[k, 1], sx.at[s, k, 1], rx.at[s, k, 1], along_x(by)
            )
        S[s][...] = total(0)

    def relay(s):
        for k, by in enumerate((1, -1)):
            x_copy[s, k, 0].wait_recv()
            XS[s][k, 2] = (YR[s][k] + XR[s][k, 0].astype(jnp.float32)).astype(jnp.bfloat16)
            x_copy[s, k, 2] = remote(
                XS[s].at[k, 2], XR[s].at[k, 2], sx.at[s, k, 2], rx.at[s, k, 2], along_x(by)
            )

    def finish(s):
        for k in range(2):
            x_copy[s, k, 1].wait_recv()
            x_copy[s, k, 2].wait_recv()
        low = S[s][:, lo] + XR[s][0, 2].astype(jnp.float32) + XR[s][1, 1].astype(jnp.float32)
        high = S[s][:, hi] + XR[s][0, 1].astype(jnp.float32) + XR[s][1, 2].astype(jnp.float32)
        live = s < counts_ref[0]
        for t in range(T0 // 2):
            span = slice(t * CH, (t + 1) * CH)
            o_ref[s, t] = jnp.where(live, low[:, span], 0.0).astype(jnp.bfloat16)
            o_ref[s, T0 // 2 + t] = jnp.where(live, high[:, span], 0.0).astype(jnp.bfloat16)

    tables.wait()
    turns.wait()
    turn_fine()
    live_count.wait()
    start_second(0)
    start_first(2)
    for c in range(CHUNKS):
        start_third(c)
        if c + 1 < CHUNKS:
            start_second(c + 1)
        if c + 3 < CHUNKS:
            start_first(c + 3)
        for chunk, begin, end in BEFORE_FOURTH[c]:
            compute_some(chunk, begin, end)
        start_fourth(c)
        for chunk, begin, end in AFTER_FOURTH[c]:
            compute_some(chunk, begin, end)
    last = LAST
    wait_finals(last)
    compute(last, 0)
    send_pair(0)
    chip_sum(0)
    compute(last, 1)
    send_pair(1)
    compute(last, 2)
    send_pair(2)
    relay(0)
    chip_sum(1)
    chip_sum(2)
    relay(1)
    finish(0)
    relay(2)
    finish(1)
    finish(2)

    for copy in list(first.values()) + list(second.values()):
        copy.wait_send()
    for copy in list(transit.values()) + list(final.values()):
        copy.wait_send()
    for copy in list(pair_copy.values()) + list(x_copy.values()):
        copy.wait_send()


def correlate(tight, spectra, requests, pairs, counts, tables, turns):
    entries = ENTRIES[tight]
    bf16, f32 = jnp.bfloat16, jnp.float32
    vmem, dma = pltpu.VMEM, pltpu.SemaphoreType.DMA
    scratch = []
    for lead in (8, 2 * entries):
        scratch += [vmem((lead, 2, CH, width), bf16) for width in WIDTHS] * W
    scratch += [vmem((2 * entries, 2, CH, width), bf16) for width in BUFFER_WIDTHS] * W
    scratch += [
        vmem((2, 8, 2, BAND), f32),
        vmem((8, 2, 128), f32),
        vmem((T1 * CH, 2 * W * max(WIDTHS)), bf16),
        vmem((T0 * CH, 2 * W * max(WIDTHS)), bf16),
        vmem((SLOTS, T1 * CH, T0 * CH), f32),
        pltpu.SMEM((W, NEED), jnp.int32),
        pltpu.SMEM((1,), jnp.int32),
    ]
    scratch += [vmem((SIDE, CH, T0 * CH), bf16)] * (2 * SLOTS)
    scratch += [vmem((CH, T0 * CH), f32)] * SLOTS
    scratch += [vmem((2, 3, CH, T0 * CH // 2), bf16)] * (2 * SLOTS)
    scratch += [vmem((2, CH, T0 * CH // 2), f32)] * SLOTS
    scratch += [
        dma((CHUNKS, W)),
        dma,
        dma,
        dma,
        dma((CHUNKS, W, 2, 2)),
        dma((CHUNKS, W, 2, 2)),
        dma((CHUNKS, W, 2)),
        dma((CHUNKS, W, 2)),
        dma((CHUNKS, W, 2, 3)),
        dma((CHUNKS, W, 2, 3)),
        dma((SLOTS, SIDE)),
        dma((SLOTS, SIDE)),
        dma((SLOTS, 2, 3)),
        dma((SLOTS, 2, 3)),
    ]
    smem = pl.BlockSpec(memory_space=pltpu.SMEM)
    hbm = pl.BlockSpec(memory_space=pl.ANY)
    out_shape = [jax.ShapeDtypeStruct((SLOTS, T0, CH, CH), bf16)]
    out_specs = [pl.BlockSpec(memory_space=pltpu.VMEM)]
    if tight:
        out_shape.append(jax.ShapeDtypeStruct((1,), jnp.int32))
        out_specs.append(smem)
    return pl.pallas_call(
        functools.partial(kernel, tight),
        out_shape=out_shape,
        in_specs=[smem, smem, hbm, hbm, hbm, hbm],
        out_specs=out_specs,
        scratch_shapes=scratch,
        compiler_params=pltpu.CompilerParams(
            collective_id=0 if tight else 1, has_side_effects=True, vmem_limit_bytes=67043328
        ),
        name="correlate_tight" if tight else "correlate_any",
    )(requests.T, pairs.transpose(0, 2, 1), counts, spectra, tables, turns)


def per_device(*operands):
    summed, fits = correlate(True, *operands)
    chosen = lax.cond(fits[0] == 1, lambda: summed, lambda: correlate(False, *operands)[0])
    return chosen.astype(jnp.float32)


def solution(mesh):
    placed = (P("tiles", None, None, None, "lag"), P(), P("tiles", None, None), P("tiles"), P(), P())
    tables, turns = phase_tables()
    mapped = jax.shard_map(
        per_device,
        mesh=mesh,
        in_specs=placed,
        out_specs=P("tiles", "lag", None, None),
        check_vma=False,
    )

    def run(spectra, requests, pairs, counts):
        return mapped(spectra, requests, pairs, counts, jnp.asarray(tables), jnp.asarray(turns))

    return run
```
